128 devices in a mesh: seq: 8 (over z, y_hi), chan: 16 (over y_lo, x, core).
Axes of the slice: x: 4, y: 4 (y_hi: 2, y_lo: 2; y = y_hi * 2 + y_lo), z: 4, core: 2. Of those that a mesh axis runs over, the one named last changes fastest.
Arguments:
- tokens: bfloat16 [4096, 4096], P('seq', 'chan'), may hold values from -6 to 6
- gate_proj: bfloat16 [4096, 8192], P(None, 'chan'), may hold values from -0.09375 to 0.09375
- value_proj: bfloat16 [4096, 8192], P(None, 'chan'), may hold values from -0.09375 to 0.09375
- state_proj: bfloat16 [4096, 256], replicated, may hold values from -0.0078125 to 0.0078125
- step_proj: bfloat16 [4096, 64], P(None, 'chan'), may hold values from -0.09375 to 0.09375
- step_bias: float32 [64], P('chan'), may hold values from -1 to 1
- decay_rate: float32 [64], P('chan'), may hold values from 0.0001 to 0.05
- skip_gain: float32 [64], P('chan'), may hold values from 0.5 to 4
- conv_kernel: float32 [4, 8192], P(None, 'chan'), may hold values from -3 to 3
- norm_gain: float32 [8192], P('chan'), may hold values from 0.1 to 1.9
- out_proj: bfloat16 [8192, 4096], P('chan'), may hold values from -0.046875 to 0.046875
- complement: int32 [4096], replicated, may hold values from 0 to 4095, as said below
- keep_mask: int32 [4096, 4096], P('seq', 'chan'), may hold values 0 or 1
Outputs:
- mixed: bfloat16 [4096, 4096], P('seq', 'chan')
The draws below stay inside these ranges and needn't reach their ends.
Inputs may be any that keep to these rules, and one draw needn't show every extreme that they name: complement pairs the features: complement[complement[j]] = j and complement[j] != j for every j.
All inputs are finite; a program needn't handle non-finite values. No bound on the sum of `keep_mask` on one device may be relied on, other than what follows from the above.
Results may differ from the reference program's by a relative error of at most 0.025.
Values may be sent and summed in bfloat16 or wider, within the bound.
No kernel may reach another device: no remote copies, remote signals or barrier semaphores. Data moves between devices by JAX's collectives and lax.ppermute only.
A program may use at most 128 MiB of HBM per device.

```python
import math
import jax
import jax.numpy as jnp
from jax import lax

D = 4096
H = 64
P_SIZE = 128
N = 128
KW = 4
BLOCK = 256
DI = 8192
TOKENS = 4096


def draw_complement(key, part):
    order = jax.random.permutation(jax.random.fold_in(key, 17), jnp.arange(D, dtype=jnp.int32))
    pairs = order.reshape(D // 2, 2)
    paired = jnp.zeros((D,), jnp.int32).at[pairs[:, 0]].set(pairs[:, 1])
    paired = paired.at[pairs[:, 1]].set(pairs[:, 0])
    return paired


def set_ends(result, own_key, low, largest):
    place = [jax.random.randint(jax.random.fold_in(own_key, axis), (), 0, length) for axis, length in enumerate(result.shape)]
    longest = result.shape.index(max(result.shape))
    neighbour = place[:longest] + [(place[longest] + 1) % result.shape[longest]] + place[longest + 1:]
    return result.at[tuple(place)].set(low).at[tuple(neighbour)].set(largest)


def block_scale(own_key, dims, split, smallest, high):
    loudness, own = 1.0, jax.random.fold_in(own_key, 6)
    for dim, shards_of in split:
        heights = jnp.exp(jax.random.uniform(jax.random.fold_in(own, dim), (shards_of,), jnp.float32, smallest / len(split), high / len(split)))
        loudness = loudness * jnp.repeat(heights, dims[dim] // shards_of).reshape([-1 if axis == dim else 1 for axis in range(len(dims))])
    return loudness


def normal_values(stream_key, dims, width, reach, cuts=(), kind=jnp.bfloat16):
    drawn = width * jax.random.normal(stream_key, dims, jnp.float32)
    if cuts:
        drawn = drawn * block_scale(stream_key, dims, cuts, -0.22, 0.18)
    return jnp.clip(drawn, -reach, reach).astype(kind)


def setup_inputs(seed: int = 0) -> dict:
    key_of = jax.random.split(jax.random.key(seed), 14)
    tokens = normal_values(key_of[0], (TOKENS, D), 1.0, 6.0, ((0, 8), (1, 16)))
    gate_proj = normal_values(key_of[1], (D, DI), D ** -0.5, 0.09375, ((1, 16),))
    value_proj = normal_values(key_of[2], (D, DI), D ** -0.5, 0.09375, ((1, 16),))
    state_proj = normal_values(key_of[3], (D, 2 * N), (D * N) ** -0.5, 0.0078125)
    step_proj = normal_values(key_of[4], (D, H), D ** -0.5, 0.09375, ((1, 16),))
    step_bias = jnp.clip(jax.random.uniform(key_of[5], (H,), jnp.float32, -1.0, 1.0) * block_scale(key_of[5], (H,), ((0, 16),), -0.4, 0.0), -1.0, 1.0)
    decay_rate = jnp.clip(jnp.exp(math.log(0.05) - 6.214608 * jax.random.uniform(key_of[6], (H,), jnp.float32) ** block_scale(key_of[6], (H,), ((0, 16),), -0.2, 0.2)), 0.0001, 0.05)
    skip_gain = jnp.clip(jnp.exp(math.log(4.0) - 2.0794415 * jax.random.uniform(key_of[7], (H,), jnp.float32) ** block_scale(key_of[7], (H,), ((0, 16),), -0.2, 0.2)), 0.5, 4.0)
    conv_kernel = normal_values(key_of[8], (KW, DI), 0.5, 3.0, ((1, 16),), jnp.float32)
    norm_gain = jnp.clip(1.0 + 0.18 * jax.random.normal(key_of[9], (DI,), jnp.float32), 0.1, 1.9)
    out_proj = normal_values(key_of[10], (DI, D), (2 * H * P_SIZE) ** -0.5, 0.046875, ((0, 16),))
    complement = draw_complement(jax.random.fold_in(key_of[13], 71), 0)
    keep_mask = set_ends((jax.random.randint(key_of[12], (TOKENS, D), 0, 10) < 9).astype(jnp.int32), jax.random.fold_in(key_of[12], 1), 0, 1)
    return dict(tokens=tokens, gate_proj=gate_proj, value_proj=value_proj, state_proj=state_proj, step_proj=step_proj, step_bias=step_bias, decay_rate=decay_rate, skip_gain=skip_gain, conv_kernel=conv_kernel, norm_gain=norm_gain, out_proj=out_proj, complement=complement, keep_mask=keep_mask)


def block_step(state, items):
    x_heads, b_part, c_part, step, log_decay = items
    cumulative = jnp.cumsum(log_decay, axis=1)
    gaps = cumulative[:, :, None, :] - cumulative[:, None, :, :]
    length = cumulative.shape[1]
    lower_mask = (jnp.arange(length)[:, None] >= jnp.arange(length)[None, :])[None, :, :, None]
    weights = jnp.where(lower_mask, jnp.exp(jnp.where(lower_mask, gaps, 0.0)), 0.0)
    x_float = x_heads.astype(jnp.float32)
    b_float = b_part.astype(jnp.float32)
    c_float = c_part.astype(jnp.float32)
    highest = lax.Precision.HIGHEST
    scores = jnp.einsum('btn,bsn->bts', c_float, b_float, precision=highest)
    mixing = weights * scores[..., None] * step[:, None, :, :]
    inner_y = jnp.einsum('btsh,bshp->bthp', mixing, x_float, precision=highest)
    carried = jnp.exp(cumulative)[..., None] * jnp.einsum('btn,bhpn->bthp', c_float, state, precision=highest)
    total_decay = cumulative[:, -1, :]
    towards = jnp.exp(total_decay[:, None, :] - cumulative) * step
    fresh = jnp.einsum('bsh,bshp,bsn->bhpn', towards, x_float, b_float, precision=highest)
    new_state = jnp.exp(total_decay)[:, :, None, None] * state + fresh
    return (new_state, inner_y + carried)

def ssd_blocks(x_heads, b_part, c_part, step, log_decay):
    branches, length, heads, head_dim = x_heads.shape
    nblocks = length // BLOCK

    def blocked(arr):
        return jnp.moveaxis(arr.reshape((branches, nblocks, BLOCK) + arr.shape[2:]), 1, 0)
    start_state = jnp.zeros((branches, heads, head_dim, b_part.shape[-1]), jnp.float32)
    end_state, outputs = lax.scan(block_step, start_state, (blocked(x_heads), blocked(b_part), blocked(c_part), blocked(step), blocked(log_decay)))
    return (jnp.moveaxis(outputs, 0, 1).reshape(x_heads.shape), end_state)

def reference(tokens, gate_proj, value_proj, state_proj, step_proj, step_bias, decay_rate, skip_gain, conv_kernel, norm_gain, out_proj, complement, keep_mask):
    inner = gate_proj.shape[1]
    heads = step_proj.shape[1]
    head_dim = inner // heads
    nstate = state_proj.shape[1] // 2
    length = tokens.shape[0]

    def project(inputs):
        gate_part = jnp.dot(inputs, gate_proj, preferred_element_type=jnp.float32).astype(jnp.bfloat16)
        value_part = jnp.dot(inputs, value_proj, preferred_element_type=jnp.float32).astype(jnp.bfloat16)
        state_part = jnp.dot(inputs, state_proj, preferred_element_type=jnp.float32).astype(jnp.bfloat16)
        step_raw = jnp.dot(inputs, step_proj, preferred_element_type=jnp.float32)
        return (gate_part, value_part, state_part, step_raw)
    forward = project(tokens)
    reverse = project(jnp.take(tokens, complement, axis=1)[::-1])
    gate_part, value_part, state_part, step_raw = [jnp.stack([a, b]) for a, b in zip(forward, reverse)]
    padded = jnp.concatenate([jnp.zeros((2, KW - 1, inner), jnp.float32), value_part.astype(jnp.float32)], axis=1)
    conv = conv_kernel[0] * padded[:, 0:length, :]
    for tap in range(1, KW):
        conv = conv + conv_kernel[tap] * padded[:, tap:tap + length, :]
    x_ssm = jax.nn.silu(conv).astype(jnp.bfloat16)
    step = jax.nn.softplus(step_raw + step_bias)
    log_decay = -step * decay_rate
    x_heads = x_ssm.reshape(2, length, heads, head_dim)
    local_y, end_state = ssd_blocks(x_heads, state_part[..., :nstate], state_part[..., nstate:], step, log_decay)
    full_y = local_y + skip_gain[:, None] * x_heads.astype(jnp.float32)
    gated = full_y * jax.nn.silu(gate_part.astype(jnp.float32).reshape(2, length, heads, head_dim))
    scale = lax.rsqrt(lax.optimization_barrier(jnp.mean(gated * gated, axis=-1, keepdims=True)) + 1e-05)
    normed = (gated * scale * norm_gain.reshape(heads, head_dim)).reshape(2, length, inner).astype(jnp.bfloat16)
    stacked = jnp.concatenate([normed[0], normed[1][::-1]], axis=1)
    out_table = jnp.concatenate([out_proj, jnp.take(out_proj, complement, axis=1)], axis=0)
    total = jnp.dot(stacked, out_table, preferred_element_type=jnp.float32)
    return (total * keep_mask.astype(jnp.float32) * (1.0 / 0.9)).astype(jnp.bfloat16)
```

```python
import jax
import jax.numpy as jnp
from jax import lax
from jax.experimental import pallas as pl
from jax.experimental.pallas import tpu as pltpu
from jax.sharding import PartitionSpec as P

BF = jnp.bfloat16
F32 = jnp.float32
KW = 4
VMEM_LIMIT = 48 * 2**20


def chip_route(dy, dx):
    return [
        ((y * 4 + x) * 2 + c, ((y + dy) % 2 * 4 + (x + dx) % 4) * 2 + c)
        for y in range(2)
        for x in range(4)
        for c in range(2)
    ]


def to_chip(a, dy, dx):
    return lax.ppermute(a, "chan", chip_route(dy, dx))


def to_sibling(a):
    return lax.ppermute(a, "chan", [(i, i ^ 1) for i in range(16)])


def dot(a, b, dims=((1,), (0,)), precision=None):
    return lax.dot_general(
        a, b, (dims, ((), ())), preferred_element_type=F32, precision=precision
    )


def params():
    return pltpu.CompilerParams(vmem_limit_bytes=VMEM_LIMIT)


def cost(flops, nbytes):
    return pl.CostEstimate(flops=int(flops), bytes_accessed=int(nbytes), transcendentals=0)


def gather_stage(blocks, chans, comp, before, gate_proj, value_proj, small_proj):
    nb = len(blocks)
    rows, width = blocks[0].shape
    d = comp.shape[1]
    tile = 512
    ntiles = d // tile
    ws = small_proj.shape[1]
    first = before is None

    def kernel(chan, *refs):
        tok = refs[:nb]
        comp_ref, gate_hbm, value_hbm, small_hbm = refs[nb : nb + 4]
        pos = nb + 4
        if not first:
            tp_in, av_in, ag_in, as_in = refs[pos : pos + 4]
            pos += 4
        tp_out, av, ag, asm = refs[pos : pos + 4]
        wg, wv, wsm, sem = refs[pos + 4 :]
        n = pl.program_id(0)

        def copies():
            out = []
            for j in range(nb):
                src = pl.ds(pl.multiple_of(chan[j] * width, width), width)
                dst = pl.ds(j * width, width)
                out.append(pltpu.make_async_copy(gate_hbm.at[src, :], wg.at[dst, :], sem.at[0, j]))
                out.append(pltpu.make_async_copy(value_hbm.at[src, :], wv.at[dst, :], sem.at[1, j]))
                out.append(pltpu.make_async_copy(small_hbm.at[src, :], wsm.at[dst, :], sem.at[2, j]))
            return out

        @pl.when(n == 0)
        def _():
            for c in copies():
                c.start()

        @pl.when(n < ntiles)
        def _():
            target = comp_ref[...]
            total = None
            for j in range(nb):
                local = target - chan[j] * width
                pick = lax.broadcasted_iota(jnp.int32, (width, tile), 0) == local
                part = dot(tok[j][...], jnp.where(pick, 1.0, 0.0).astype(BF))
                total = part if total is None else total + part
            if not first:
                total = total + tp_in[...].astype(F32)
            tp_out[...] = total.astype(BF)

        @pl.when(n == ntiles)
        def _():
            for c in copies():
                c.wait()
            x = jnp.concatenate([tok[j][...] for j in range(nb)], axis=1)
            if first:
                av[...] = dot(x, wv[...])
                ag[...] = dot(x, wg[...])
                asm[...] = dot(x, wsm[...])
            else:
                av[...] = dot(x, wv[...]) + av_in[...]
                ag[...] = dot(x, wg[...]) + ag_in[...]
                asm[...] = dot(x, wsm[...]) + as_in[...]

    inner = gate_proj.shape[1]
    whole = lambda shape: pl.BlockSpec(shape, lambda n, s: (0,) * len(shape))
    tp_spec = pl.BlockSpec((rows, tile), lambda n, s: (0, jnp.minimum(n, ntiles - 1)))
    any_spec = pl.BlockSpec(memory_space=pl.ANY)
    acc_specs = [tp_spec, whole((rows, inner)), whole((rows, inner)), whole((rows, ws))]
    shapes = [
        jax.ShapeDtypeStruct((rows, d), BF),
        jax.ShapeDtypeStruct((rows, inner), F32),
        jax.ShapeDtypeStruct((rows, inner), F32),
        jax.ShapeDtypeStruct((rows, ws), F32),
    ]
    args = [chans, *blocks, comp, gate_proj, value_proj, small_proj]
    in_specs = [whole((rows, width))] * nb
    in_specs += [pl.BlockSpec((1, tile), lambda n, s: (0, jnp.minimum(n, ntiles - 1)))]
    in_specs += [any_spec] * 3
    aliases = {}
    if not first:
        aliases = {len(args) + i: i for i in range(4)}
        args += before
        in_specs += acc_specs
    return pl.pallas_call(
        kernel,
        grid_spec=pltpu.PrefetchScalarGridSpec(
            num_scalar_prefetch=1,
            grid=(ntiles + 1,),
            in_specs=in_specs,
            out_specs=acc_specs,
            scratch_shapes=[
                pltpu.VMEM((nb * width, inner), BF),
                pltpu.VMEM((nb * width, inner), BF),
                pltpu.VMEM((nb * width, ws), BF),
                pltpu.SemaphoreType.DMA((3, nb)),
            ],
        ),
        out_shape=shapes,
        input_output_aliases=aliases,
        compiler_params=params(),
        cost_estimate=cost(2 * rows * nb * width * (d + 2 * inner + ws), 8 * 2**20),
        name="gather_stage",
    )(*args)


def reverse_small(tp, value_proj, small_proj, acc_value, acc_small):
    rows, d = tp.shape
    inner, ws = value_proj.shape[1], small_proj.shape[1]
    kb = 512

    def kernel(t, wv, wsm, av, asm, v_out, bc_out, st_out, accv, accs):
        i = pl.program_id(0)

        @pl.when(i == 0)
        def _():
            accv[...] = jnp.zeros_like(accv)
            accs[...] = jnp.zeros_like(accs)

        accv[...] += dot(t[...], wv[...])
        accs[...] += dot(t[...], wsm[...])

        @pl.when(i == d // kb - 1)
        def _():
            v_out[0] = av[...].astype(BF)
            v_out[1] = accv[...].astype(BF)
            bc_out[0] = asm[:, :256].astype(BF)
            bc_out[1] = accs[:, :256].astype(BF)
            st_out[0] = asm[:, 256:]
            st_out[1] = accs[:, 256:]

    whole = lambda shape: pl.BlockSpec(shape, lambda i: (0,) * len(shape))
    return pl.pallas_call(
        kernel,
        grid=(d // kb,),
        in_specs=[
            pl.BlockSpec((rows, kb), lambda i: (0, i)),
            pl.BlockSpec((kb, inner), lambda i: (i, 0)),
            pl.BlockSpec((kb, ws), lambda i: (i, 0)),
            whole((rows, inner)),
            whole((rows, ws)),
        ],
        out_specs=[whole((2, rows, inner)), whole((2, rows, 256)), whole((2, rows, 128))],
        out_shape=[
            jax.ShapeDtypeStruct((2, rows, inner), BF),
            jax.ShapeDtypeStruct((2, rows, 256), BF),
            jax.ShapeDtypeStruct((2, rows, 128), F32),
        ],
        scratch_shapes=[pltpu.VMEM((rows, inner), F32), pltpu.VMEM((rows, ws), F32)],
        compiler_params=params(),
        cost_estimate=cost(2 * rows * d * (inner + ws), 12 * 2**20),
        name="reverse_small",
    )(tp, value_proj, small_proj, acc_value, acc_small)


def reverse_gate(tp, gate_proj, acc_gate):
    rows, d = tp.shape
    inner = gate_proj.shape[1]
    kb = 512

    def kernel(t, wg, ag, g_out, acc):
        i = pl.program_id(0)

        @pl.when(i == 0)
        def _():
            acc[...] = jnp.zeros_like(acc)
            g_out[0] = ag[...].astype(BF)

        acc[...] += dot(t[...], wg[...])

        @pl.when(i == d // kb - 1)
        def _():
            g_out[1] = acc[...].astype(BF)

    whole = lambda shape: pl.BlockSpec(shape, lambda i: (0,) * len(shape))
    return pl.pallas_call(
        kernel,
        grid=(d // kb,),
        in_specs=[
            pl.BlockSpec((rows, kb), lambda i: (0, i)),
            pl.BlockSpec((kb, inner), lambda i: (i, 0)),
            whole((rows, inner)),
        ],
        out_specs=whole((2, rows, inner)),
        out_shape=jax.ShapeDtypeStruct((2, rows, inner), BF),
        scratch_shapes=[pltpu.VMEM((rows, inner), F32)],
        compiler_params=params(),
        cost_estimate=cost(2 * rows * d * inner, 10 * 2**20),
        name="reverse_gate",
    )(tp, gate_proj, acc_gate)


def steps(raw, bias, rate):
    _, rows, lanes = raw.shape

    def kernel(raw_ref, bias_ref, rate_ref, step_o, cum_o, step_t, cum_t, decay_o):
        r = lax.broadcasted_iota(jnp.int32, (rows, rows), 0)
        c = lax.broadcasted_iota(jnp.int32, (rows, rows), 1)
        for b in range(2):
            step = jax.nn.softplus(raw_ref[b] + bias_ref[...])
            logdec = -step * rate_ref[...]
            tri = jnp.where((r >= c) if b == 0 else (r <= c), 1.0, 0.0)
            cum = dot(tri, logdec, precision=lax.Precision.HIGHEST)
            step_o[b] = step
            cum_o[b] = cum
            step_t[b] = step.T[:8]
            cum_t[b] = cum.T[:8]
            last = cum[rows - 1 : rows] if b == 0 else cum[0:1]
            decay_o[b : b + 1] = jnp.exp(last)

    vm = pl.BlockSpec(memory_space=pltpu.VMEM)
    return pl.pallas_call(
        kernel,
        in_specs=[vm] * 3,
        out_specs=[vm] * 5,
        out_shape=[
            jax.ShapeDtypeStruct((2, rows, lanes), F32),
            jax.ShapeDtypeStruct((2, rows, lanes), F32),
            jax.ShapeDtypeStruct((2, 8, rows), F32),
            jax.ShapeDtypeStruct((2, 8, rows), F32),
            jax.ShapeDtypeStruct((2, lanes), F32),
        ],
        compiler_params=params(),
        cost_estimate=cost(10**9, 2**20),
        name="steps",
    )(raw, bias, rate)


def conv_states(value, halo, taps, bc, step, cum):
    _, rows, inner = value.shape
    heads = inner // 128

    def kernel(v_ref, halo_ref, taps_ref, bc_ref, step_ref, cum_ref, xs_o, end_o):
        def branch(b):
            v = v_ref[0].astype(F32)
            hal = halo_ref[0].astype(F32)
            if b == 0:
                padded = jnp.concatenate([hal, v], axis=0)
                shift = lambda k: padded[5 + k : 5 + k + rows]
            else:
                padded = jnp.concatenate([v, hal], axis=0)
                shift = lambda k: padded[3 - k : 3 - k + rows]
            conv = taps_ref[0:1] * shift(0)
            for k in range(1, KW):
                conv = conv + taps_ref[k : k + 1] * shift(k)
            xs = (conv * jax.nn.sigmoid(conv)).astype(BF)
            xs_o[0] = xs
            cums = cum_ref[0]
            last = cums[rows - 1 : rows] if b == 0 else cums[0:1]
            towards = jnp.exp(last - cums) * step_ref[0]
            bm = bc_ref[0].astype(F32)
            for h in range(heads):
                weighted = (bm * towards[:, h : h + 1]).astype(BF)
                end_o[0, h] = dot(weighted, xs[:, h * 128 : h * 128 + 128], ((0,), (0,)))

        for b in range(2):
            pl.when(pl.program_id(0) == b)(lambda b=b: branch(b))

    by = lambda *shape: pl.BlockSpec((1, *shape), lambda b: (b,) + (0,) * len(shape))
    return pl.pallas_call(
        kernel,
        grid=(2,),
        in_specs=[
            by(rows, inner),
            by(8, inner),
            pl.BlockSpec(taps.shape, lambda b: (0, 0)),
            by(rows, 128),
            by(rows, 128),
            by(rows, 128),
        ],
        out_specs=[by(rows, inner), by(heads, 128, 128)],
        out_shape=[
            jax.ShapeDtypeStruct((2, rows, inner), BF),
            jax.ShapeDtypeStruct((2, heads, 128, 128), F32),
        ],
        compiler_params=params(),
        cost_estimate=cost(10**9, 3 * 2**20),
        name="conv_states",
    )(value, halo, taps, bc, step, cum)


def within_shard(xs, bc, step_t, cum_t, cum, skip):
    _, rows, inner = xs.shape
    heads = inner // 128
    half = rows // 2

    def kernel(x_ref, bc_ref, st_ref, ct_ref, cum_ref, skip_ref, y_ref):
        h = pl.program_id(1)
        lane = lax.broadcasted_iota(jnp.int32, (1, 128), 1)
        pick = lane == h
        cum_col = jnp.sum(jnp.where(pick, cum_ref[0], 0.0), axis=1, keepdims=True)
        gain = jnp.sum(jnp.where(pick, skip_ref[...], 0.0), axis=1, keepdims=True)
        cum_row = ct_ref[0, pl.ds(h, 1), :]
        step_row = st_ref[0, pl.ds(h, 1), :]
        lower = lax.broadcasted_iota(jnp.int32, (half, half), 0) >= lax.broadcasted_iota(
            jnp.int32, (half, half), 1
        )
        upper = lax.broadcasted_iota(jnp.int32, (half, half), 0) <= lax.broadcasted_iota(
            jnp.int32, (half, half), 1
        )

        def part(t, s, mask):
            ts, ss = slice(t * half, t * half + half), slice(s * half, s * half + half)
            gap = jnp.minimum(cum_col[ts] - cum_row[:, ss], 0.0)
            w = jnp.exp(gap)
            if mask is not None:
                w = jnp.where(mask, w, 0.0)
            scores = dot(bc_ref[0, ts, 128:], bc_ref[0, ss, :128], ((1,), (1,)))
            mixing = (w * scores * step_row[:, ss]).astype(BF)
            return dot(mixing, x_ref[0, ss, :])

        def branch(b):
            early, late = (0, 1) if b == 0 else (1, 0)
            mask = lower if b == 0 else upper
            for t, y in (
                (early, part(early, early, mask)),
                (late, part(late, late, mask) + part(late, early, None)),
            ):
                ts = slice(t * half, t * half + half)
                y_ref[0, ts, :] = y + gain * x_ref[0, ts, :].astype(F32)

        for b in range(2):
            pl.when(pl.program_id(0) == b)(lambda b=b: branch(b))

    by = lambda *shape: pl.BlockSpec((1, *shape), lambda b, h: (b,) + (0,) * len(shape))
    head = pl.BlockSpec((1, rows, 128), lambda b, h: (b, 0, h))
    return pl.pallas_call(
        kernel,
        grid=(2, heads),
        in_specs=[
            head,
            by(rows, 256),
            by(8, rows),
            by(8, rows),
            by(rows, 128),
            pl.BlockSpec((1, 128), lambda b, h: (0, 0)),
        ],
        out_specs=head,
        out_shape=jax.ShapeDtypeStruct((2, rows, inner), F32),
        compiler_params=params(),
        cost_estimate=cost(4 * 10**9, 4 * 2**20),
        name="within_shard",
    )(xs, bc, step_t, cum_t, cum, skip)


def finish(local_y, incoming, bc, cum, gate, norm_gain):
    _, rows, inner = local_y.shape
    heads = inner // 128

    def kernel(y_ref, s_ref, bc_ref, cum_ref, g_ref, gain_ref, o_ref):
        h = pl.program_id(1)
        lane = lax.broadcasted_iota(jnp.int32, (1, 128), 1)
        cum_col = jnp.sum(jnp.where(lane == h, cum_ref[0], 0.0), axis=1, keepdims=True)
        entering = dot(bc_ref[0], s_ref[0, 0])
        y = y_ref[0] + jnp.exp(cum_col) * entering
        g = g_ref[0].astype(F32)
        gated = y * (g * jax.nn.sigmoid(g))
        scale = lax.rsqrt(jnp.mean(gated * gated, axis=-1, keepdims=True) + 1e-05)
        o_ref[...] = (gated * scale * gain_ref[...]).astype(BF)

    by = lambda *shape: pl.BlockSpec((1, *shape), lambda b, h: (b,) + (0,) * len(shape))
    head = pl.BlockSpec((1, rows, 128), lambda b, h: (b, 0, h))
    return pl.pallas_call(
        kernel,
        grid=(2, heads),
        in_specs=[
            head,
            pl.BlockSpec((1, 1, 128, 128), lambda b, h: (b, h, 0, 0)),
            pl.BlockSpec((1, rows, 128), lambda b, h: (b, 0, 1)),
            by(rows, 128),
            head,
            pl.BlockSpec((1, 128), lambda b, h: (0, h)),
        ],
        out_specs=pl.BlockSpec((rows, 128), lambda b, h: (0, b * heads + h)),
        out_shape=jax.ShapeDtypeStruct((rows, 2 * inner), BF),
        compiler_params=params(),
        cost_estimate=cost(10**9, 5 * 2**20),
        name="finish",
    )(local_y, incoming, bc, cum, gate, norm_gain)


def output_table(comp, out_proj):
    inner, d = out_proj.shape
    r = 512
    nb = d // r
    tiles = inner // 128

    def kernel(idx, o_ref, plain_o, perm_o, rows_f32, picked):
        i = pl.program_id(0)

        @pl.when(i < nb)
        def _():
            r0 = pl.multiple_of(i * r * tiles, r * tiles)
            for j in range(tiles):
                t = o_ref[128 * j : 128 * j + 128, :].astype(F32).T
                rows_f32[pl.ds(r0 + j, r, tiles), :] = t
                plain_o[:, 128 * j : 128 * j + 128] = t.astype(BF)

        @pl.when(i >= nb)
        def _():
            b0 = (i - nb) * r

            def body(n, _):
                for k in range(16):
                    row = n * 16 + k
                    src = pl.multiple_of(idx[b0 + row] * tiles, tiles)
                    dst = pl.multiple_of(row * tiles, tiles)
                    picked[pl.ds(dst, tiles), :] = rows_f32[pl.ds(src, tiles), :]
                return 0

            lax.fori_loop(0, r // 16, body, 0)
            for j in range(tiles):
                perm_o[:, 128 * j : 128 * j + 128] = picked[pl.ds(j, r, tiles), :].astype(BF)

    return pl.pallas_call(
        kernel,
        grid_spec=pltpu.PrefetchScalarGridSpec(
            num_scalar_prefetch=1,
            grid=(2 * nb,),
            in_specs=[pl.BlockSpec((inner, r), lambda i, s: (0, jnp.minimum(i, nb - 1)))],
            out_specs=[
                pl.BlockSpec((r, inner), lambda i, s: (jnp.minimum(i, nb - 1), 0)),
                pl.BlockSpec((r, inner), lambda i, s: (jnp.maximum(i - nb, 0), 0)),
            ],
            scratch_shapes=[
                pltpu.VMEM((d * tiles, 128), F32),
                pltpu.VMEM((r * tiles, 128), F32),
            ],
        ),
        out_shape=[jax.ShapeDtypeStruct((d, inner), BF)] * 2,
        compiler_params=params(),
        cost_estimate=cost(8 * 10**9, 12 * 2**20),
        name="output_table",
    )(comp, out_proj)


def output_stage(order, mine, others, plain, perm, plain_sib, perm_sib):
    rows, twice = mine.shape
    inner = twice // 2
    n = order.shape[0] // 2
    cols = 256

    def kernel(idx, a, b, p0, q0, p1, q1, o_ref):
        nt = ((1,), (1,))
        o_ref[0] = (
            dot(a[:, :inner], p0[...], nt)
            + dot(a[:, inner:], q0[...], nt)
            + dot(b[:, :inner], p1[...], nt)
            + dot(b[:, inner:], q1[...], nt)
        )

    own = pl.BlockSpec((cols, inner), lambda i, s: (s[2 * i], 0))
    sib = pl.BlockSpec((cols, inner), lambda i, s: (s[2 * i + 1], 0))
    whole = pl.BlockSpec((rows, twice), lambda i, s: (0, 0))
    return pl.pallas_call(
        kernel,
        grid_spec=pltpu.PrefetchScalarGridSpec(
            num_scalar_prefetch=1,
            grid=(n,),
            in_specs=[whole, whole, own, own, sib, sib],
            out_specs=pl.BlockSpec((1, rows, cols), lambda i, s: (i, 0, 0)),
        ),
        out_shape=jax.ShapeDtypeStruct((n, rows, cols), F32),
        compiler_params=params(),
        cost_estimate=cost(n * 4 * rows * twice * cols, n * 2 * 2**20),
        name="output_stage",
    )(order, mine, others, plain, perm, plain_sib, perm_sib)


def split(a):
    high = a.astype(BF)
    return high, (a - high.astype(F32)).astype(BF)


def join(high, low):
    return high.astype(F32) + low.astype(F32)


def halo_exchange(value, decay):
    rows = value.shape[1]
    fh, fl = split(decay)
    tail = jnp.stack([fh[0], fl[0], fh[1], fl[1]])
    tail = jnp.pad(tail, ((0, 1), (0, value.shape[2] - 128)))
    down = jnp.concatenate([value[0, rows - 3 :], tail], axis=0)
    up = jnp.concatenate([value[1, :3], tail], axis=0)
    from_below = lax.ppermute(down, "seq", [(i, i + 1) for i in range(7)])
    from_above = lax.ppermute(up, "seq", [(i + 1, i) for i in range(7)])
    return from_below, from_above


def shards(
    tokens,
    gate_proj,
    value_proj,
    state_proj,
    step_proj,
    step_bias,
    decay_rate,
    skip_gain,
    conv_kernel,
    norm_gain,
    out_proj,
    complement,
    keep_mask,
):
    rows, width = tokens.shape
    inner = gate_proj.shape[1]
    heads = step_proj.shape[1]
    d = gate_proj.shape[0]
    place = lax.axis_index("chan")
    core, chip = place % 2, place // 2
    y, x = chip // 4, chip % 4
    seq = lax.axis_index("seq")
    z, half = seq // 2, seq % 2

    def chip_at(dy, dx):
        return (y + dy) % 2 * 4 + (x + dx) % 4

    def lanes(a):
        return jnp.pad(a, (0, 128 - heads)).reshape(1, 128)

    comp = complement.reshape(1, d)
    small_proj = jnp.concatenate(
        [state_proj, step_proj, jnp.zeros((d, 128 - heads), BF)], axis=1
    )

    weights = (gate_proj, value_proj, small_proj)

    def stage(parts, before):
        blocks, chans = [], []
        for block, sib, dy, dx in parts:
            blocks += [block, sib]
            chans += [2 * chip_at(dy, dx) + core, 2 * chip_at(dy, dx) + 1 - core]
        return gather_stage(
            blocks, jnp.stack(chans).astype(jnp.int32), comp, before, *weights
        )

    own = tokens
    a = to_chip(own, 0, 1)
    b = to_chip(own, 0, -1)
    c = to_chip(own, 1, 0)
    own_s = to_sibling(own)
    acc = stage([(own, own_s, 0, 0)], None)
    a_s, b_s, c_s = to_sibling(a), to_sibling(b), to_sibling(c)
    dd = to_chip(a, 1, 0)
    e = to_chip(c, 0, -1)
    f = to_chip(a, 0, 1)
    acc = stage([(a, a_s, 0, -1), (b, b_s, 0, 1), (c, c_s, 1, 0)], acc)
    third = (168, 336)
    g = jnp.concatenate(
        [
            to_chip(dd[: third[0]], 0, 1),
            to_chip(e[third[0] : third[1]], 0, -1),
            to_chip(f[third[1] :], 1, 0),
        ]
    )
    d_s, e_s, f_s = to_sibling(dd), to_sibling(e), to_sibling(f)
    acc = stage([(dd, d_s, 1, -1), (e, e_s, 1, 1), (f, f_s, 0, 2)], acc)
    g_s = to_sibling(g)
    tp, acc_v, acc_g, acc_s = stage([(g, g_s, 1, 2)], acc)

    value, bc, raw = reverse_small(tp, value_proj, small_proj, acc_v, acc_s)
    step, cum, step_t, cum_t, decay = steps(raw, lanes(step_bias), lanes(decay_rate))
    below, above = halo_exchange(value, decay)
    zeros5 = jnp.zeros((5, inner), BF)
    halo = jnp.stack(
        [
            jnp.concatenate([zeros5, below[:3]], axis=0),
            jnp.concatenate([above[:3], zeros5], axis=0),
        ]
    )
    pair_msg = jnp.where(half == 0, above[3:7, :128], below[3:7, :128])
    pair = jnp.stack([join(pair_msg[0], pair_msg[1]), join(pair_msg[2], pair_msg[3])])
    xs, end = conv_states(value, halo, conv_kernel, bc, step, cum)

    d0 = jnp.where(half == 0, decay, pair)[:, :heads]
    d1 = jnp.where(half == 0, pair, decay)[:, :heads]

    def message(branch):
        parts = [*split(d0[branch]), *split(d1[branch])]
        rows4 = jnp.stack([jnp.pad(v, (0, 128 - heads)) for v in parts])
        rows4 = jnp.pad(rows4, ((0, 12), (0, 0)))
        return jnp.concatenate([end[branch].astype(BF).reshape(heads * 128, 128), rows4])

    msg_f, msg_b = message(0), message(1)
    got = []
    for k in range(1, 4):
        route = [(zz * 2 + hh, (zz + k) % 4 * 2 + hh) for zz in range(4) for hh in range(2)]
        got.append(lax.ppermute(jnp.where(z + k < 4, msg_f, msg_b), "seq", route))

    def opened(m):
        st = m[: heads * 128].astype(F32).reshape(heads, 128, 128)
        t = m[heads * 128 : heads * 128 + 4, :heads]
        return st, join(t[0], t[1]), join(t[2], t[3])

    opened_msgs = [opened(m) for m in got]
    wide = lambda v: v[:, None, None]

    def partial_sum(branch):
        total = jnp.zeros((heads, 128, 128), F32)
        passed = jnp.ones((heads,), F32)
        for j in range(1, 4):
            st, e0, e1 = opened_msgs[j - 1] if branch == 0 else opened_msgs[3 - j]
            valid = (z >= j) if branch == 0 else (z + j < 4)
            own_step = jnp.where(half == 0, e1, 1.0) if branch == 0 else jnp.where(half == 1, e0, 1.0)
            total = total + jnp.where(valid, wide(passed * own_step) * st, 0.0)
            passed = jnp.where(valid, passed * e0 * e1, passed)
        return total

    pf, pb = partial_sum(0), partial_sum(1)
    d0f, d1b = wide(d0[0]), wide(d1[1])
    send_f = jnp.where(half == 0, d0f * pf + end[0], pf)
    send_b = jnp.where(half == 1, d1b * pb + end[1], pb)
    recv = lax.ppermute(
        jnp.stack([send_f, send_b]).astype(BF), "seq", [(i, i ^ 1) for i in range(8)]
    ).astype(F32)
    in_f = jnp.where(half == 0, pf, d0f * pf) + recv[0]
    in_b = jnp.where(half == 1, pb, d1b * pb) + recv[1]
    incoming = jnp.stack([in_f, in_b]).astype(BF)

    gate = reverse_gate(tp, gate_proj, acc_g)
    local_y = within_shard(xs, bc, step_t, cum_t, cum, lanes(skip_gain))
    plain, perm = output_table(complement, out_proj)
    for_sib = lambda t: lax.dynamic_index_in_dim(
        t.reshape(8, 2, 256, inner), 1 - core, 1, False
    ).reshape(8 * 256, inner)
    plain_sib, perm_sib = to_sibling(for_sib(plain)), to_sibling(for_sib(perm))

    normed = finish(local_y, incoming, bc, cum, gate, norm_gain.reshape(1, inner))
    others = to_sibling(normed)

    def shares(*offsets):
        order = []
        for dy, dx in offsets:
            order += [2 * chip_at(dy, dx) + core, chip_at(dy, dx)]
        order = jnp.stack(order).astype(jnp.int32)
        return output_stage(order, normed, others, plain, perm, plain_sib, perm_sib)

    far = shares((1, 2))[0].astype(BF)
    r_a = to_chip(far[: third[0]], 0, 1)
    r_b = to_chip(far[third[0] : third[1]], 0, -1)
    r_c = to_chip(far[third[1] :], 1, 0)
    mid = shares((1, 1), (1, -1), (0, 2))
    m_a = mid[0].at[: third[0]].add(r_a.astype(F32)).astype(BF)
    m_b = mid[1].at[third[0] : third[1]].add(r_b.astype(F32)).astype(BF)
    m_c = mid[2].at[third[1] :].add(r_c.astype(F32)).astype(BF)
    s_a = to_chip(m_a, 1, 0)
    s_b = to_chip(m_b, 0, -1)
    s_c = to_chip(m_c, 0, 1)
    near = shares((0, 1), (0, -1), (1, 0), (0, 0))
    n_a = (near[0] + s_a.astype(F32) + s_c.astype(F32)).astype(BF)
    n_b = near[1].astype(BF)
    n_c = (near[2] + s_b.astype(F32)).astype(BF)
    t_a = to_chip(n_a, 0, 1).astype(F32)
    t_b = to_chip(n_b, 0, -1).astype(F32)
    t_c = to_chip(n_c, 1, 0).astype(F32)
    summed = near[3] + t_a + t_b + t_c
    return (summed * keep_mask.astype(F32) * (1.0 / 0.9)).astype(BF)


def solution(mesh):
    return jax.shard_map(
        shards,
        mesh=mesh,
        in_specs=(
            P("seq", "chan"),
            P(None, "chan"),
            P(None, "chan"),
            P(),
            P(None, "chan"),
            P("chan"),
            P("chan"),
            P("chan"),
            P(None, "chan"),
            P("chan"),
            P("chan", None),
            P(),
            P("seq", "chan"),
        ),
        out_specs=P("seq", "chan"),
        check_vma=False,
    )
```

```python
import jax
import jax.numpy as jnp
from jax import lax
from jax.experimental import pallas as pl
from jax.experimental.pallas import tpu as pltpu
from jax.sharding import PartitionSpec as P

BF = jnp.bfloat16
F32 = jnp.float32
KW = 4


def chip_route(dy, dx):
    return [
        ((y * 4 + x) * 2 + c, ((y + dy) % 2 * 4 + (x + dx) % 4) * 2 + c)
        for y in range(2)
        for x in range(4)
        for c in range(2)
    ]


def to_chip(a, dy, dx):
    return lax.ppermute(a, "chan", chip_route(dy, dx))


def to_sibling(a):
    return lax.ppermute(a, "chan", [(i, i ^ 1) for i in range(16)])


def dot(a, b, dims=((1,), (0,)), precision=None):
    return lax.dot_general(
        a, b, (dims, ((), ())), preferred_element_type=F32, precision=precision
    )


def params(mib=24):
    return pltpu.CompilerParams(vmem_limit_bytes=mib * 2**20)


def cost(flops, nbytes):
    return pl.CostEstimate(flops=int(flops), bytes_accessed=int(nbytes), transcendentals=0)


def project(blocks, chans, comp, gate_proj, value_proj, state_proj, step_t, bias, rate):
    nb = len(blocks)
    rows, width = blocks[0].shape
    d = comp.shape[0]
    inner = gate_proj.shape[1]
    ns = state_proj.shape[1]
    heads = step_t.shape[0]
    tiles = rows // 128

    def kernel(chan, idx, *refs):
        tok = refs[:nb]
        wg_hbm, wv_hbm, ws_hbm, st_ref, bias_ref, rate_ref = refs[nb : nb + 6]
        v_out, g_out, bc_out, step_o, cum_o, step_to, cum_to, decay_o = refs[nb + 6 : nb + 14]
        t, tp, by_row, picked, wg, wv, ws, sem, wsem = refs[nb + 14 :]

        def token_copy(j, at):
            return pltpu.make_async_copy(tok[j], t.at[:, pl.ds(at, width)], sem.at[j])

        weight_copies = [
            pltpu.make_async_copy(a, b, wsem.at[i])
            for i, (a, b) in enumerate([(ws_hbm, ws.at[:, :ns]), (wv_hbm, wv), (wg_hbm, wg)])
        ]
        for j in range(nb):
            token_copy(j, pl.multiple_of(chan[j] * width, width)).start()
        for c in weight_copies:
            c.start()
        st = st_ref[...].astype(F32)
        wst = jnp.concatenate([st, jnp.zeros((128 - heads, d), F32)], axis=0).T
        ws[:, ns:] = wst.astype(BF)

        for j in range(nb):
            at = pl.multiple_of(chan[j] * width, width)
            token_copy(j, at).wait()
            for k in range(tiles):
                part = t[128 * k : 128 * k + 128, pl.ds(at, width)].astype(F32).T
                by_row[pl.ds(at * tiles + k, width, tiles), :] = part

        def permute(c, _):
            b0 = c * width

            def body(n, _):
                for k in range(32):
                    row = n * 32 + k
                    src = pl.multiple_of(idx[b0 + row], tiles)
                    dst = pl.multiple_of(row * tiles, tiles)
                    picked[pl.ds(dst, tiles), :] = by_row[pl.ds(src, tiles), :]
                return 0

            lax.fori_loop(0, width // 32, body, 0)
            for k in range(tiles):
                part = picked[pl.ds(k, width, tiles), :].T
                tp[128 * k : 128 * k + 128, pl.ds(pl.multiple_of(b0, width), width)] = part.astype(BF)
            return 0

        lax.fori_loop(0, d // width, permute, 0)
        weight_copies[0].wait()
        r = lax.broadcasted_iota(jnp.int32, (rows, rows), 0)
        q = lax.broadcasted_iota(jnp.int32, (rows, rows), 1)
        for b, u in enumerate((t, tp)):
            small = dot(u[...], ws[...])
            bc_out[b] = small[:, :ns].astype(BF)
            step = jax.nn.softplus(small[:, ns:] + bias_ref[...])
            tri = jnp.where((r >= q) if b == 0 else (r <= q), 1.0, 0.0).astype(BF)
            logdec = -step * rate_ref[...]
            high = logdec.astype(BF)
            rest = logdec - high.astype(F32)
            mid = rest.astype(BF)
            low = (rest - mid.astype(F32)).astype(BF)
            sums = dot(tri, jnp.concatenate([high, mid, low], axis=1))
            cum = sums[:, :128] + sums[:, 128:256] + sums[:, 256:]
            step_o[b] = step
            cum_o[b] = cum
            step_to[b] = step.T[:8]
            cum_to[b] = cum.T[:8]
            decay_o[b : b + 1] = jnp.exp(cum[rows - 1 : rows] if b == 0 else cum[0:1])
        weight_copies[1].wait()
        for b, u in enumerate((t, tp)):
            v_out[b] = dot(u[...], wv[...]).astype(BF)
        weight_copies[2].wait()
        for b, u in enumerate((t, tp)):
            g_out[b] = dot(u[...], wg[...]).astype(BF)

    shapes = [
        jax.ShapeDtypeStruct((2, rows, inner), BF),
        jax.ShapeDtypeStruct((2, rows, inner), BF),
        jax.ShapeDtypeStruct((2, rows, ns), BF),
        jax.ShapeDtypeStruct((2, rows, 128), F32),
        jax.ShapeDtypeStruct((2, rows, 128), F32),
        jax.ShapeDtypeStruct((2, 8, rows), F32),
        jax.ShapeDtypeStruct((2, 8, rows), F32),
        jax.ShapeDtypeStruct((2, 128), F32),
    ]
    whole = lambda shape: pl.BlockSpec(shape, lambda n, s, i: (0,) * len(shape))
    any_spec = pl.BlockSpec(memory_space=pl.ANY)
    return pl.pallas_call(
        kernel,
        grid_spec=pltpu.PrefetchScalarGridSpec(
            num_scalar_prefetch=2,
            grid=(1,),
            in_specs=[any_spec] * (nb + 3) + [whole((heads, d)), whole((1, 128)), whole((1, 128))],
            out_specs=[whole(o.shape) for o in shapes],
            scratch_shapes=[
                pltpu.VMEM((rows, d), BF),
                pltpu.VMEM((rows, d), BF),
                pltpu.VMEM((d * tiles, 128), F32),
                pltpu.VMEM((width * tiles, 128), F32),
                pltpu.VMEM((d, inner), BF),
                pltpu.VMEM((d, inner), BF),
                pltpu.VMEM((d, ns + 128), BF),
                pltpu.SemaphoreType.DMA((nb,)),
                pltpu.SemaphoreType.DMA((3,)),
            ],
        ),
        out_shape=shapes,
        compiler_params=params(60),
        cost_estimate=cost(4 * rows * d * (2 * inner + 512), 20 * 2**20),
        name="project",
    )(chans, comp * tiles, *blocks, gate_proj, value_proj, state_proj, step_t, bias, rate)


def conv_states(value, halo, taps, bc, step, cum):
    _, rows, inner = value.shape
    heads = inner // 128

    def kernel(v_ref, halo_ref, taps_ref, bc_ref, step_ref, cum_ref, xs_o, end_o):
        def branch(b):
            v = v_ref[0].astype(F32)
            hal = halo_ref[0].astype(F32)
            if b == 0:
                padded = jnp.concatenate([hal, v], axis=0)
                shift = lambda k: padded[5 + k : 5 + k + rows]
            else:
                padded = jnp.concatenate([v, hal], axis=0)
                shift = lambda k: padded[3 - k : 3 - k + rows]
            conv = taps_ref[0:1] * shift(0)
            for k in range(1, KW):
                conv = conv + taps_ref[k : k + 1] * shift(k)
            xs = (conv * jax.nn.sigmoid(conv)).astype(BF)
            xs_o[0] = xs
            cums = cum_ref[0]
            last = cums[rows - 1 : rows] if b == 0 else cums[0:1]
            towards = jnp.exp(last - cums) * step_ref[0]
            bm = bc_ref[0].astype(F32)
            for h in range(heads):
                weighted = (bm * towards[:, h : h + 1]).astype(BF)
                end_o[0, h] = dot(weighted, xs[:, h * 128 : h * 128 + 128], ((0,), (0,)))

        for b in range(2):
            pl.when(pl.program_id(0) == b)(lambda b=b: branch(b))

    by = lambda *shape: pl.BlockSpec((1, *shape), lambda b: (b,) + (0,) * len(shape))
    return pl.pallas_call(
        kernel,
        grid=(2,),
        in_specs=[
            by(rows, inner),
            by(8, inner),
            pl.BlockSpec(taps.shape, lambda b: (0, 0)),
            by(rows, 128),
            by(rows, 128),
            by(rows, 128),
        ],
        out_specs=[by(rows, inner), by(heads, 128, 128)],
        out_shape=[
            jax.ShapeDtypeStruct((2, rows, inner), BF),
            jax.ShapeDtypeStruct((2, heads, 128, 128), F32),
        ],
        compiler_params=params(24),
        cost_estimate=cost(10**9, 3 * 2**20),
        name="conv_states",
    )(value, halo, taps, bc, step, cum)


def within_shard(xs, bc, step_t, cum_t, cum, skip):
    _, rows, inner = xs.shape
    heads = inner // 128
    half = rows // 2

    def kernel(x_ref, bc_ref, st_ref, ct_ref, cum_ref, skip_ref, y_ref):
        h = pl.program_id(1)
        lane = lax.broadcasted_iota(jnp.int32, (1, 128), 1)
        pick = lane == h
        cum_col = jnp.sum(jnp.where(pick, cum_ref[0], 0.0), axis=1, keepdims=True)
        gain = jnp.sum(jnp.where(pick, skip_ref[...], 0.0), axis=1, keepdims=True)
        cum_row = ct_ref[0, pl.ds(h, 1), :]
        step_row = st_ref[0, pl.ds(h, 1), :]
        lower = lax.broadcasted_iota(jnp.int32, (half, half), 0) >= lax.broadcasted_iota(
            jnp.int32, (half, half), 1
        )
        upper = lax.broadcasted_iota(jnp.int32, (half, half), 0) <= lax.broadcasted_iota(
            jnp.int32, (half, half), 1
        )

        def part(t, s, mask):
            ts, ss = slice(t * half, t * half + half), slice(s * half, s * half + half)
            gap = jnp.minimum(cum_col[ts] - cum_row[:, ss], 0.0)
            w = jnp.exp(gap)
            if mask is not None:
                w = jnp.where(mask, w, 0.0)
            scores = dot(bc_ref[0, ts, 128:], bc_ref[0, ss, :128], ((1,), (1,)))
            mixing = (w * scores * step_row[:, ss]).astype(BF)
            return dot(mixing, x_ref[0, ss, :])

        def branch(b):
            early, late = (0, 1) if b == 0 else (1, 0)
            mask = lower if b == 0 else upper
            for t, y in (
                (early, part(early, early, mask)),
                (late, part(late, late, mask) + part(late, early, None)),
            ):
                ts = slice(t * half, t * half + half)
                y_ref[0, ts, :] = y + gain * x_ref[0, ts, :].astype(F32)

        for b in range(2):
            pl.when(pl.program_id(0) == b)(lambda b=b: branch(b))

    by = lambda *shape: pl.BlockSpec((1, *shape), lambda b, h: (b,) + (0,) * len(shape))
    head = pl.BlockSpec((1, rows, 128), lambda b, h: (b, 0, h))
    return pl.pallas_call(
        kernel,
        grid=(2, heads),
        in_specs=[
            head,
            by(rows, 256),
            by(8, rows),
            by(8, rows),
            by(rows, 128),
            pl.BlockSpec((1, 128), lambda b, h: (0, 0)),
        ],
        out_specs=head,
        out_shape=jax.ShapeDtypeStruct((2, rows, inner), F32),
        compiler_params=params(),
        cost_estimate=cost(4 * 10**9, 4 * 2**20),
        name="within_shard",
    )(xs, bc, step_t, cum_t, cum, skip)


def finish(local_y, incoming, bc, cum, gate, norm_gain):
    _, rows, inner = local_y.shape
    heads = inner // 128

    def kernel(y_ref, s_ref, bc_ref, cum_ref, g_ref, gain_ref, o_ref):
        h = pl.program_id(1)
        lane = lax.broadcasted_iota(jnp.int32, (1, 128), 1)
        cum_col = jnp.sum(jnp.where(lane == h, cum_ref[0], 0.0), axis=1, keepdims=True)
        entering = dot(bc_ref[0], s_ref[0, 0])
        y = y_ref[0] + jnp.exp(cum_col) * entering
        g = g_ref[0].astype(F32)
        gated = y * (g * jax.nn.sigmoid(g))
        scale = lax.rsqrt(jnp.mean(gated * gated, axis=-1, keepdims=True) + 1e-05)
        o_ref[...] = (gated * scale * gain_ref[...]).astype(BF)

    by = lambda *shape: pl.BlockSpec((1, *shape), lambda b, h: (b,) + (0,) * len(shape))
    head = pl.BlockSpec((1, rows, 128), lambda b, h: (b, 0, h))
    return pl.pallas_call(
        kernel,
        grid=(2, heads),
        in_specs=[
            head,
            pl.BlockSpec((1, 1, 128, 128), lambda b, h: (b, h, 0, 0)),
            pl.BlockSpec((1, rows, 128), lambda b, h: (b, 0, 1)),
            by(rows, 128),
            head,
            pl.BlockSpec((1, 128), lambda b, h: (0, h)),
        ],
        out_specs=pl.BlockSpec((rows, 128), lambda b, h: (0, b * heads + h)),
        out_shape=jax.ShapeDtypeStruct((rows, 2 * inner), BF),
        compiler_params=params(),
        cost_estimate=cost(10**9, 5 * 2**20),
        name="finish",
    )(local_y, incoming, bc, cum, gate, norm_gain)


def output_table(comp, core, out_proj):
    inner, d = out_proj.shape
    r = 512
    nb = d // r
    tiles = inner // 128
    half = r // 2

    def kernel(idx, core_ref, o_ref, plain_keep, plain_send, perm_keep, perm_send, rows_f32, picked):
        i = pl.program_id(0)
        even = core_ref[0] == 0

        def put(keep, send, j, t):
            keep[:, 128 * j : 128 * j + 128] = jnp.where(even, t[:half], t[half:]).astype(BF)
            send[:, 128 * j : 128 * j + 128] = jnp.where(even, t[half:], t[:half]).astype(BF)

        @pl.when(i < nb)
        def _():
            r0 = pl.multiple_of(i * r * tiles, r * tiles)
            for j in range(tiles):
                t = o_ref[128 * j : 128 * j + 128, :].astype(F32).T
                rows_f32[pl.ds(r0 + j, r, tiles), :] = t
                put(plain_keep, plain_send, j, t)

        @pl.when(i >= nb)
        def _():
            b0 = (i - nb) * r

            def body(n, _):
                for k in range(16):
                    row = n * 16 + k
                    src = pl.multiple_of(idx[b0 + row] * tiles, tiles)
                    dst = pl.multiple_of(row * tiles, tiles)
                    picked[pl.ds(dst, tiles), :] = rows_f32[pl.ds(src, tiles), :]
                return 0

            lax.fori_loop(0, r // 16, body, 0)
            for j in range(tiles):
                put(perm_keep, perm_send, j, picked[pl.ds(j, r, tiles), :])

    early = pl.BlockSpec((half, inner), lambda i, s, c: (jnp.minimum(i, nb - 1), 0))
    late = pl.BlockSpec((half, inner), lambda i, s, c: (jnp.maximum(i - nb, 0), 0))
    return pl.pallas_call(
        kernel,
        grid_spec=pltpu.PrefetchScalarGridSpec(
            num_scalar_prefetch=2,
            grid=(2 * nb,),
            in_specs=[pl.BlockSpec((inner, r), lambda i, s, c: (0, jnp.minimum(i, nb - 1)))],
            out_specs=[early, early, late, late],
            scratch_shapes=[
                pltpu.VMEM((d * tiles, 128), F32),
                pltpu.VMEM((r * tiles, 128), F32),
            ],
        ),
        out_shape=[jax.ShapeDtypeStruct((d // 2, inner), BF)] * 4,
        compiler_params=params(24),
        cost_estimate=cost(8 * 10**9, 12 * 2**20),
        name="output_table",
    )(comp, core, out_proj)


def output_stage(order, mine, others, tables, added, out_dtype):
    rows, twice = mine.shape
    inner = twice // 2
    n = order.shape[0]
    cols = 256
    na = len(added)

    def kernel(idx, a, b, p0, q0, p1, q1, *rest):
        o_ref = rest[na]
        nt = ((1,), (1,))
        left = jnp.concatenate([a[...], b[...]], axis=1)
        table = jnp.concatenate([p0[...], q0[...], p1[...], q1[...]], axis=1)
        total = dot(left, table, nt)
        for place in range(n):
            mask = pl.program_id(0) == place
            for (at, _), ref in zip(added, rest[:na]):
                if at == place and n == 1:
                    total = total + ref[...].astype(F32)
                elif at == place:
                    total = total + jnp.where(mask, ref[...].astype(F32), 0.0)
        o_ref[0] = total.astype(out_dtype)

    table = pl.BlockSpec((cols, inner), lambda i, s: (s[i], 0))
    whole = lambda c: pl.BlockSpec((rows, c), lambda i, s: (0, 0))
    return pl.pallas_call(
        kernel,
        grid_spec=pltpu.PrefetchScalarGridSpec(
            num_scalar_prefetch=1,
            grid=(n,),
            in_specs=[whole(twice), whole(twice)] + [table] * 4 + [whole(cols)] * na,
            out_specs=pl.BlockSpec((1, rows, cols), lambda i, s: (i, 0, 0)),
        ),
        out_shape=jax.ShapeDtypeStruct((n, rows, cols), out_dtype),
        compiler_params=params(24),
        cost_estimate=cost(n * 4 * rows * twice * cols, n * 3 * 2**20),
        name="output_stage",
    )(order, mine, others, *tables, *[v for _, v in added])


def split(a):
    high = a.astype(BF)
    return high, (a - high.astype(F32)).astype(BF)


def join(high, low):
    return high.astype(F32) + low.astype(F32)


def halo_exchange(value, decay):
    rows = value.shape[1]
    fh, fl = split(decay)
    tail = jnp.stack([fh[0], fl[0], fh[1], fl[1]])
    tail = jnp.pad(tail, ((0, 1), (0, value.shape[2] - 128)))
    down = jnp.concatenate([value[0, rows - 3 :], tail], axis=0)
    up = jnp.concatenate([value[1, :3], tail], axis=0)
    from_below = lax.ppermute(down, "seq", [(i, i + 1) for i in range(7)])
    from_above = lax.ppermute(up, "seq", [(i + 1, i) for i in range(7)])
    return from_below, from_above


def shards(
    tokens,
    gate_proj,
    value_proj,
    state_proj,
    step_proj,
    step_bias,
    decay_rate,
    skip_gain,
    conv_kernel,
    norm_gain,
    out_proj,
    complement,
    keep_mask,
):
    rows, width = tokens.shape
    inner = gate_proj.shape[1]
    heads = step_proj.shape[1]
    d = gate_proj.shape[0]
    place = lax.axis_index("chan")
    core, chip = place % 2, place // 2
    y, x = chip // 4, chip % 4
    seq = lax.axis_index("seq")
    z, half = seq // 2, seq % 2

    core1 = core.reshape(1).astype(jnp.int32)

    def chip_at(dy, dx):
        return (y + dy) % 2 * 4 + (x + dx) % 4

    def lanes(a):
        return jnp.pad(a, (0, 128 - heads)).reshape(1, 128)

    own = tokens
    a = to_chip(own, 0, 1)
    b = to_chip(own, 0, -1)
    c = to_chip(own, 1, 0)
    own_s = to_sibling(own)
    a_s, b_s, c_s = to_sibling(a), to_sibling(b), to_sibling(c)
    dd = to_chip(a, 1, 0)
    e = to_chip(c, 0, -1)
    f = to_chip(a, 0, 1)
    g = to_chip(f, 1, 0)
    d_s, e_s, f_s = to_sibling(dd), to_sibling(e), to_sibling(f)
    g_s = to_sibling(g)
    parts = [
        (own, own_s, 0, 0),
        (a, a_s, 0, -1),
        (b, b_s, 0, 1),
        (c, c_s, 1, 0),
        (dd, d_s, 1, -1),
        (e, e_s, 1, 1),
        (f, f_s, 0, 2),
        (g, g_s, 1, 2),
    ]
    blocks, chans = [], []
    for block, sib, dy, dx in parts:
        blocks += [block, sib]
        chans += [2 * chip_at(dy, dx) + core, 2 * chip_at(dy, dx) + 1 - core]
    chans = jnp.stack(chans).astype(jnp.int32)
    value, gate, bc, step, cum, step_t, cum_t, decay = project(
        blocks,
        chans,
        complement,
        gate_proj,
        value_proj,
        state_proj,
        step_proj.T,
        lanes(step_bias),
        lanes(decay_rate),
    )
    comp_after, value = lax.optimization_barrier((complement, value))
    below, above = halo_exchange(value, decay)
    table = output_table(comp_after, core1, out_proj)
    below, above, *table = lax.optimization_barrier((below, above, *table))
    plain, plain_send, perm, perm_send = table
    tables = (plain, perm, to_sibling(plain_send), to_sibling(perm_send))
    zeros5 = jnp.zeros((5, inner), BF)
    halo = jnp.stack(
        [
            jnp.concatenate([zeros5, below[:3]], axis=0),
            jnp.concatenate([above[:3], zeros5], axis=0),
        ]
    )
    pair_msg = jnp.where(half == 0, above[3:7, :128], below[3:7, :128])
    pair = jnp.stack([join(pair_msg[0], pair_msg[1]), join(pair_msg[2], pair_msg[3])])
    xs, end = conv_states(value, halo, conv_kernel, bc, step, cum)

    d0 = jnp.where(half == 0, decay, pair)[:, :heads]
    d1 = jnp.where(half == 0, pair, decay)[:, :heads]

    def message(branch):
        parts = [*split(d0[branch]), *split(d1[branch])]
        rows4 = jnp.stack([jnp.pad(v, (0, 128 - heads)) for v in parts])
        rows4 = jnp.pad(rows4, ((0, 12), (0, 0)))
        return jnp.concatenate([end[branch].astype(BF).reshape(heads * 128, 128), rows4])

    msg_f, msg_b = message(0), message(1)
    got = []
    for k in range(1, 4):
        route = [(zz * 2 + hh, (zz + k) % 4 * 2 + hh) for zz in range(4) for hh in range(2)]
        got.append(lax.ppermute(jnp.where(z + k < 4, msg_f, msg_b), "seq", route))

    def opened(m):
        st = m[: heads * 128].astype(F32).reshape(heads, 128, 128)
        t = m[heads * 128 : heads * 128 + 4, :heads]
        return st, join(t[0], t[1]), join(t[2], t[3])

    opened_msgs = [opened(m) for m in got]
    wide = lambda v: v[:, None, None]

    def partial_sum(branch):
        total = jnp.zeros((heads, 128, 128), F32)
        passed = jnp.ones((heads,), F32)
        for j in range(1, 4):
            st, e0, e1 = opened_msgs[j - 1] if branch == 0 else opened_msgs[3 - j]
            valid = (z >= j) if branch == 0 else (z + j < 4)
            own_step = jnp.where(half == 0, e1, 1.0) if branch == 0 else jnp.where(half == 1, e0, 1.0)
            total = total + jnp.where(valid, wide(passed * own_step) * st, 0.0)
            passed = jnp.where(valid, passed * e0 * e1, passed)
        return total

    pf, pb = partial_sum(0), partial_sum(1)
    d0f, d1b = wide(d0[0]), wide(d1[1])
    send_f = jnp.where(half == 0, d0f * pf + end[0], pf)
    send_b = jnp.where(half == 1, d1b * pb + end[1], pb)
    recv = lax.ppermute(
        jnp.stack([send_f, send_b]).astype(BF), "seq", [(i, i ^ 1) for i in range(8)]
    ).astype(F32)
    in_f = jnp.where(half == 0, pf, d0f * pf) + recv[0]
    in_b = jnp.where(half == 1, pb, d1b * pb) + recv[1]
    incoming = jnp.stack([in_f, in_b]).astype(BF)

    local_y = within_shard(xs, bc, step_t, cum_t, cum, lanes(skip_gain))
    normed = finish(local_y, incoming, bc, cum, gate, norm_gain.reshape(1, inner))
    others = to_sibling(normed)

    def shares(offsets, added=(), out_dtype=BF):
        order = jnp.stack([chip_at(dy, dx) for dy, dx in offsets]).astype(jnp.int32)
        return output_stage(order, normed, others, tables, added, out_dtype)

    r = to_chip(shares([(1, 2)])[0], 1, 0)
    s_a = to_chip(shares([(1, 1)])[0], 1, 0)
    s_b = to_chip(shares([(1, -1)])[0], 0, -1)
    s_c = to_chip(shares([(0, 2)], [(0, r)])[0], 0, 1)
    t_b = to_chip(shares([(0, -1)])[0], 0, -1)
    here = shares([(0, 0)], out_dtype=F32)[0]
    t_c = to_chip(shares([(1, 0)], [(0, s_b)])[0], 1, 0)
    t_a = to_chip(shares([(0, 1)], [(0, s_a), (0, s_c)])[0], 0, 1)
    summed = here + t_a.astype(F32) + t_b.astype(F32) + t_c.astype(F32)
    return (summed * keep_mask.astype(F32) * (1.0 / 0.9)).astype(BF)


def solution(mesh):
    return jax.shard_map(
        shards,
        mesh=mesh,
        in_specs=(
            P("seq", "chan"),
            P(None, "chan"),
            P(None, "chan"),
            P(),
            P(None, "chan"),
            P("chan"),
            P("chan"),
            P("chan"),
            P(None, "chan"),
            P("chan"),
            P("chan", None),
            P(),
            P("seq", "chan"),
        ),
        out_specs=P("seq", "chan"),
        check_vma=False,
    )
```

```python
import jax
import jax.numpy as jnp
from jax import lax
from jax.experimental import pallas as pl
from jax.experimental.pallas import tpu as pltpu
from jax.sharding import PartitionSpec as P

BF = jnp.bfloat16
F32 = jnp.float32
KW = 4


def chip_route(dy, dx):
    return [
        ((y * 4 + x) * 2 + c, ((y + dy) % 2 * 4 + (x + dx) % 4) * 2 + c)
        for y in range(2)
        for x in range(4)
        for c in range(2)
    ]


def to_chip(a, dy, dx):
    return lax.ppermute(a, "chan", chip_route(dy, dx))


def to_sibling(a):
    return lax.ppermute(a, "chan", [(i, i ^ 1) for i in range(16)])


def dot(a, b, dims=((1,), (0,)), precision=None):
    return lax.dot_general(
        a, b, (dims, ((), ())), preferred_element_type=F32, precision=precision
    )


def params(mib=24):
    return pltpu.CompilerParams(vmem_limit_bytes=mib * 2**20)


def cost(flops, nbytes):
    return pl.CostEstimate(flops=int(flops), bytes_accessed=int(nbytes), transcendentals=0)


def lanes(ref):
    row = ref[...]
    return jnp.concatenate([row, jnp.zeros((1, 128 - row.shape[1]), F32)], axis=1)


def project(blocks, offsets, place, comp, gate_proj, value_proj, state_proj, step_t, bias, rate):
    nb = len(blocks)
    rows, width = blocks[0].shape
    d = comp.shape[0]
    inner = gate_proj.shape[1]
    ns = state_proj.shape[1]
    heads = step_t.shape[0]
    tiles = rows // 128

    def kernel(place_ref, idx, *refs):
        chan = place_ref
        tok = refs[:nb]
        wg_hbm, wv_hbm, ws_hbm, st_ref, bias_ref, rate_ref = refs[nb : nb + 6]
        v_out, g_out, bc_out, step_o, cum_o, step_to, cum_to, decay_o, down_o, up_o = refs[nb + 6 : nb + 16]
        t, tp, by_row, picked, wg, wv, ws, sem, wsem = refs[nb + 16 :]

        def token_copy(j, at):
            return pltpu.make_async_copy(tok[j], t.at[:, pl.ds(at, width)], sem.at[j])

        weight_copies = [
            pltpu.make_async_copy(a, b, wsem.at[i])
            for i, (a, b) in enumerate([(ws_hbm, ws.at[:, :ns]), (wv_hbm, wv), (wg_hbm, wg)])
        ]
        for j in range(nb):
            token_copy(j, pl.multiple_of(chan[j] * width, width)).start()
        for c in weight_copies:
            c.start()
        st = st_ref[...].astype(F32)
        wst = jnp.concatenate([st, jnp.zeros((128 - heads, d), F32)], axis=0).T
        ws[:, ns:] = wst.astype(BF)

        for j in range(nb):
            at = pl.multiple_of(chan[j] * width, width)
            token_copy(j, at).wait()
            for k in range(tiles):
                part = t[128 * k : 128 * k + 128, pl.ds(at, width)].astype(F32).T
                by_row[pl.ds(at * tiles + k, width, tiles), :] = part

        def permute(c, _):
            b0 = c * width

            def body(n, _):
                for k in range(32):
                    row = n * 32 + k
                    src = pl.multiple_of(idx[b0 + row] * tiles, tiles)
                    dst = pl.multiple_of(row * tiles, tiles)
                    picked[pl.ds(dst, tiles), :] = by_row[pl.ds(src, tiles), :]
                return 0

            lax.fori_loop(0, width // 32, body, 0)
            for k in range(tiles):
                part = picked[pl.ds(k, width, tiles), :].T
                tp[128 * k : 128 * k + 128, pl.ds(pl.multiple_of(b0, width), width)] = part.astype(BF)
            return 0

        lax.fori_loop(0, d // width, permute, 0)
        weight_copies[0].wait()
        r = lax.broadcasted_iota(jnp.int32, (rows, rows), 0)
        q = lax.broadcasted_iota(jnp.int32, (rows, rows), 1)
        decays = []
        for b, u in enumerate((t, tp)):
            small = dot(u[...], ws[...])
            bc_out[b] = small[:, :ns].astype(BF)
            step = jax.nn.softplus(small[:, ns:] + lanes(bias_ref))
            tri = jnp.where((r >= q) if b == 0 else (r <= q), 1.0, 0.0).astype(BF)
            logdec = -step * lanes(rate_ref)
            high = logdec.astype(BF)
            rest = logdec - high.astype(F32)
            mid = rest.astype(BF)
            low = (rest - mid.astype(F32)).astype(BF)
            sums = dot(tri, jnp.concatenate([high, mid, low], axis=1))
            cum = sums[:, :128] + sums[:, 128:256] + sums[:, 256:]
            step_o[b] = step
            cum_o[b] = cum
            step_to[b] = step.T[:8]
            cum_to[b] = cum.T[:8]
            decay = jnp.exp(cum[rows - 1 : rows] if b == 0 else cum[0:1])
            decay_o[b : b + 1] = decay
            decays += [decay, decay - decay.astype(BF).astype(F32)]
        weight_copies[1].wait()
        row8 = lax.broadcasted_iota(jnp.int32, (8, inner), 0)
        for b, u in enumerate((t, tp)):
            v = dot(u[...], wv[...])
            v_out[b] = v.astype(BF)
            message = pltpu.roll(v[rows - 8 :], 3, 0) if b == 0 else v[:8]
            for i, part in enumerate(decays):
                wide = jnp.concatenate([part, jnp.zeros((1, inner - 128), F32)], axis=1)
                message = jnp.where(row8 == 3 + i, wide, message)
            (down_o if b == 0 else up_o)[...] = message.astype(BF)
        weight_copies[2].wait()
        for b, u in enumerate((t, tp)):
            g_out[b] = dot(u[...], wg[...]).astype(BF)

    shapes = [
        jax.ShapeDtypeStruct((2, rows, inner), BF),
        jax.ShapeDtypeStruct((2, rows, inner), BF),
        jax.ShapeDtypeStruct((2, rows, ns), BF),
        jax.ShapeDtypeStruct((2, rows, 128), F32),
        jax.ShapeDtypeStruct((2, rows, 128), F32),
        jax.ShapeDtypeStruct((2, 8, rows), F32),
        jax.ShapeDtypeStruct((2, 8, rows), F32),
        jax.ShapeDtypeStruct((2, 128), F32),
        jax.ShapeDtypeStruct((8, inner), BF),
        jax.ShapeDtypeStruct((8, inner), BF),
    ]
    whole = lambda shape: pl.BlockSpec(shape, lambda n, s, i: (0,) * len(shape))
    any_spec = pl.BlockSpec(memory_space=pl.ANY)
    return pl.pallas_call(
        kernel,
        grid_spec=pltpu.PrefetchScalarGridSpec(
            num_scalar_prefetch=2,
            grid=(1,),
            in_specs=[any_spec] * (nb + 3) + [whole((heads, d)), whole((1, heads)), whole((1, heads))],
            out_specs=[whole(o.shape) for o in shapes],
            scratch_shapes=[
                pltpu.VMEM((rows, d), BF),
                pltpu.VMEM((rows, d), BF),
                pltpu.VMEM((d * tiles, 128), F32),
                pltpu.VMEM((width * tiles, 128), F32),
                pltpu.VMEM((d, inner), BF),
                pltpu.VMEM((d, inner), BF),
                pltpu.VMEM((d, ns + 128), BF),
                pltpu.SemaphoreType.DMA((nb,)),
                pltpu.SemaphoreType.DMA((3,)),
            ],
        ),
        out_shape=shapes,
        compiler_params=params(60),
        cost_estimate=cost(4 * rows * d * (2 * inner + 512), 20 * 2**20),
        name="project",
    )(place, comp, *blocks, gate_proj, value_proj, state_proj, step_t, bias, rate)


def conv_states(value, below, above, taps, bc, step, cum):
    _, rows, inner = value.shape
    heads = inner // 128

    def kernel(v_ref, below_ref, above_ref, taps_ref, bc_ref, step_ref, cum_ref, xs_o, end_o):
        def branch(b):
            v = v_ref[0].astype(F32)
            if b == 0:
                padded = jnp.concatenate([pltpu.roll(below_ref[...].astype(F32), 5, 0), v], axis=0)
                shift = lambda k: padded[5 + k : 5 + k + rows]
            else:
                padded = jnp.concatenate([v, above_ref[...].astype(F32)], axis=0)
                shift = lambda k: padded[3 - k : 3 - k + rows]
            conv = taps_ref[0:1] * shift(0)
            for k in range(1, KW):
                conv = conv + taps_ref[k : k + 1] * shift(k)
            xs = (conv * jax.nn.sigmoid(conv)).astype(BF)
            xs_o[0] = xs
            cums = cum_ref[0]
            last = cums[rows - 1 : rows] if b == 0 else cums[0:1]
            towards = jnp.exp(last - cums) * step_ref[0]
            bm = bc_ref[0].astype(F32)
            for h in range(heads):
                weighted = (bm * towards[:, h : h + 1]).astype(BF)
                end_o[0, h] = dot(weighted, xs[:, h * 128 : h * 128 + 128], ((0,), (0,)))

        for b in range(2):
            pl.when(pl.program_id(0) == b)(lambda b=b: branch(b))

    by = lambda *shape: pl.BlockSpec((1, *shape), lambda b: (b,) + (0,) * len(shape))
    return pl.pallas_call(
        kernel,
        grid=(2,),
        in_specs=[
            by(rows, inner),
            pl.BlockSpec((8, inner), lambda b: (0, 0)),
            pl.BlockSpec((8, inner), lambda b: (0, 0)),
            pl.BlockSpec(taps.shape, lambda b: (0, 0)),
            by(rows, 128),
            by(rows, 128),
            by(rows, 128),
        ],
        out_specs=[by(rows, inner), by(heads, 128, 128)],
        out_shape=[
            jax.ShapeDtypeStruct((2, rows, inner), BF),
            jax.ShapeDtypeStruct((2, heads, 128, 128), F32),
        ],
        compiler_params=params(24),
        cost_estimate=cost(10**9, 3 * 2**20),
        name="conv_states",
    )(value, below, above, taps, bc, step, cum)


def within_shard(xs, bc, step_t, cum_t, cum, skip):
    _, rows, inner = xs.shape
    heads = inner // 128
    half = rows // 2

    def kernel(x_ref, bc_ref, st_ref, ct_ref, cum_ref, skip_ref, y_ref):
        h = pl.program_id(1)
        lane = lax.broadcasted_iota(jnp.int32, (1, 128), 1)
        pick = lane == h
        cum_col = jnp.sum(jnp.where(pick, cum_ref[0], 0.0), axis=1, keepdims=True)
        gain = jnp.sum(jnp.where(pick, lanes(skip_ref), 0.0), axis=1, keepdims=True)
        cum_row = ct_ref[0, pl.ds(h, 1), :]
        step_row = st_ref[0, pl.ds(h, 1), :]
        lower = lax.broadcasted_iota(jnp.int32, (half, half), 0) >= lax.broadcasted_iota(
            jnp.int32, (half, half), 1
        )
        upper = lax.broadcasted_iota(jnp.int32, (half, half), 0) <= lax.broadcasted_iota(
            jnp.int32, (half, half), 1
        )

        def part(t, s, mask):
            ts, ss = slice(t * half, t * half + half), slice(s * half, s * half + half)
            gap = jnp.minimum(cum_col[ts] - cum_row[:, ss], 0.0)
            w = jnp.exp(gap)
            if mask is not None:
                w = jnp.where(mask, w, 0.0)
            scores = dot(bc_ref[0, ts, 128:], bc_ref[0, ss, :128], ((1,), (1,)))
            mixing = (w * scores * step_row[:, ss]).astype(BF)
            return dot(mixing, x_ref[0, ss, :])

        def branch(b):
            early, late = (0, 1) if b == 0 else (1, 0)
            mask = lower if b == 0 else upper
            for t, y in (
                (early, part(early, early, mask)),
                (late, part(late, late, mask) + part(late, early, None)),
            ):
                ts = slice(t * half, t * half + half)
                y_ref[0, ts, :] = y + gain * x_ref[0, ts, :].astype(F32)

        for b in range(2):
            pl.when(pl.program_id(0) == b)(lambda b=b: branch(b))

    by = lambda *shape: pl.BlockSpec((1, *shape), lambda b, h: (b,) + (0,) * len(shape))
    head = pl.BlockSpec((1, rows, 128), lambda b, h: (b, 0, h))
    return pl.pallas_call(
        kernel,
        grid=(2, heads),
        in_specs=[
            head,
            by(rows, 256),
            by(8, rows),
            by(8, rows),
            by(rows, 128),
            pl.BlockSpec((1, heads), lambda b, h: (0, 0)),
        ],
        out_specs=head,
        out_shape=jax.ShapeDtypeStruct((2, rows, inner), F32),
        compiler_params=params(),
        cost_estimate=cost(4 * 10**9, 4 * 2**20),
        name="within_shard",
    )(xs, bc, step_t, cum_t, cum, skip)


def finish(local_y, incoming, bc, cum, gate, norm_gain):
    _, rows, inner = local_y.shape
    heads = inner // 128

    def kernel(y_ref, s_ref, bc_ref, cum_ref, g_ref, gain_ref, o_ref):
        h = pl.program_id(1)
        lane = lax.broadcasted_iota(jnp.int32, (1, 128), 1)
        cum_col = jnp.sum(jnp.where(lane == h, cum_ref[0], 0.0), axis=1, keepdims=True)
        entering = dot(bc_ref[0], s_ref[0, 0])
        y = y_ref[0] + jnp.exp(cum_col) * entering
        g = g_ref[0].astype(F32)
        gated = y * (g * jax.nn.sigmoid(g))
        scale = lax.rsqrt(jnp.mean(gated * gated, axis=-1, keepdims=True) + 1e-05)
        o_ref[...] = (gated * scale * gain_ref[...]).astype(BF)

    by = lambda *shape: pl.BlockSpec((1, *shape), lambda b, h: (b,) + (0,) * len(shape))
    head = pl.BlockSpec((1, rows, 128), lambda b, h: (b, 0, h))
    return pl.pallas_call(
        kernel,
        grid=(2, heads),
        in_specs=[
            head,
            pl.BlockSpec((1, 1, 128, 128), lambda b, h: (b, h, 0, 0)),
            pl.BlockSpec((1, rows, 128), lambda b, h: (b, 0, 1)),
            by(rows, 128),
            head,
            pl.BlockSpec((1, 128), lambda b, h: (0, h)),
        ],
        out_specs=pl.BlockSpec((rows, 128), lambda b, h: (0, b * heads + h)),
        out_shape=jax.ShapeDtypeStruct((rows, 2 * inner), BF),
        compiler_params=params(),
        cost_estimate=cost(10**9, 5 * 2**20),
        name="finish",
    )(local_y, incoming, bc, cum, gate, norm_gain)


def output_table(comp, core, out_proj):
    inner, d = out_proj.shape
    r = 512
    nb = d // r
    tiles = inner // 128
    half = r // 2

    def kernel(idx, core_ref, o_ref, plain_keep, plain_send, perm_keep, perm_send, rows_f32, picked):
        i = pl.program_id(0)
        even = core_ref[0] == 0

        def put(keep, send, j, t):
            keep[:, 128 * j : 128 * j + 128] = jnp.where(even, t[:half], t[half:]).astype(BF)
            send[:, 128 * j : 128 * j + 128] = jnp.where(even, t[half:], t[:half]).astype(BF)

        @pl.when(i < nb)
        def _():
            r0 = pl.multiple_of(i * r * tiles, r * tiles)
            for j in range(tiles):
                t = o_ref[128 * j : 128 * j + 128, :].astype(F32).T
                rows_f32[pl.ds(r0 + j, r, tiles), :] = t
                put(plain_keep, plain_send, j, t)

        @pl.when(i >= nb)
        def _():
            b0 = (i - nb) * r

            def body(n, _):
                for k in range(16):
                    row = n * 16 + k
                    src = pl.multiple_of(idx[b0 + row] * tiles, tiles)
                    dst = pl.multiple_of(row * tiles, tiles)
                    picked[pl.ds(dst, tiles), :] = rows_f32[pl.ds(src, tiles), :]
                return 0

            lax.fori_loop(0, r // 16, body, 0)
            for j in range(tiles):
                put(perm_keep, perm_send, j, picked[pl.ds(j, r, tiles), :])

    early = pl.BlockSpec((half, inner), lambda i, s, c: (jnp.minimum(i, nb - 1), 0))
    late = pl.BlockSpec((half, inner), lambda i, s, c: (jnp.maximum(i - nb, 0), 0))
    return pl.pallas_call(
        kernel,
        grid_spec=pltpu.PrefetchScalarGridSpec(
            num_scalar_prefetch=2,
            grid=(2 * nb,),
            in_specs=[pl.BlockSpec((inner, r), lambda i, s, c: (0, jnp.minimum(i, nb - 1)))],
            out_specs=[early, early, late, late],
            scratch_shapes=[
                pltpu.VMEM((d * tiles, 128), F32),
                pltpu.VMEM((r * tiles, 128), F32),
            ],
        ),
        out_shape=[jax.ShapeDtypeStruct((d // 2, inner), BF)] * 4,
        compiler_params=params(24),
        cost_estimate=cost(8 * 10**9, 12 * 2**20),
        name="output_table",
    )(comp, core, out_proj)


def output_stage(order, mine, others, tables, added, out_dtype):
    rows, twice = mine.shape
    inner = twice // 2
    n = order.shape[0]
    cols = 256
    na = len(added)

    def kernel(idx, a, b, p0, q0, p1, q1, *rest):
        o_ref = rest[na]
        nt = ((1,), (1,))
        left = jnp.concatenate([a[...], b[...]], axis=1)
        table = jnp.concatenate([p0[...], q0[...], p1[...], q1[...]], axis=1)
        total = dot(left, table, nt)
        for place in range(n):
            mask = pl.program_id(0) == place
            for (at, _), ref in zip(added, rest[:na]):
                if at == place and n == 1:
                    total = total + ref[...].astype(F32)
                elif at == place:
                    total = total + jnp.where(mask, ref[...].astype(F32), 0.0)
        o_ref[0] = total.astype(out_dtype)

    table = pl.BlockSpec((cols, inner), lambda i, s: (s[i], 0))
    whole = lambda c: pl.BlockSpec((rows, c), lambda i, s: (0, 0))
    return pl.pallas_call(
        kernel,
        grid_spec=pltpu.PrefetchScalarGridSpec(
            num_scalar_prefetch=1,
            grid=(n,),
            in_specs=[whole(twice), whole(twice)] + [table] * 4 + [whole(cols)] * na,
            out_specs=pl.BlockSpec((1, rows, cols), lambda i, s: (i, 0, 0)),
        ),
        out_shape=jax.ShapeDtypeStruct((n, rows, cols), out_dtype),
        compiler_params=params(24),
        cost_estimate=cost(n * 4 * rows * twice * cols, n * 3 * 2**20),
        name="output_stage",
    )(order, mine, others, *tables, *[v for _, v in added])


def split(a):
    high = a.astype(BF)
    return high, (a - high.astype(F32)).astype(BF)


def join(high, low):
    return high.astype(F32) + low.astype(F32)


def shards(
    tokens,
    gate_proj,
    value_proj,
    state_proj,
    step_proj,
    step_bias,
    decay_rate,
    skip_gain,
    conv_kernel,
    norm_gain,
    out_proj,
    complement,
    keep_mask,
):
    rows, width = tokens.shape
    inner = gate_proj.shape[1]
    heads = step_proj.shape[1]
    d = gate_proj.shape[0]
    place = lax.axis_index("chan")
    core, chip = place % 2, place // 2
    y, x = chip // 4, chip % 4
    seq = lax.axis_index("seq")
    z, half = seq // 2, seq % 2

    core1 = core.reshape(1).astype(jnp.int32)

    def chip_at(dy, dx):
        return (y + dy) % 2 * 4 + (x + dx) % 4

    own = tokens
    a = to_chip(own, 0, 1)
    b = to_chip(own, 0, -1)
    c = to_chip(own, 1, 0)
    own_s = to_sibling(own)
    a_s, b_s, c_s = to_sibling(a), to_sibling(b), to_sibling(c)
    dd = to_chip(a, 1, 0)
    e = to_chip(c, 0, -1)
    f = to_chip(a, 0, 1)
    g = to_chip(f, 1, 0)
    d_s, e_s, f_s = to_sibling(dd), to_sibling(e), to_sibling(f)
    g_s = to_sibling(g)
    parts = [
        (own, own_s, 0, 0),
        (a, a_s, 0, -1),
        (b, b_s, 0, 1),
        (c, c_s, 1, 0),
        (dd, d_s, 1, -1),
        (e, e_s, 1, 1),
        (f, f_s, 0, 2),
        (g, g_s, 1, 2),
    ]
    blocks, offsets = [], []
    for block, sib, dy, dx in parts:
        blocks += [block, sib]
        offsets += [(dy, dx, 0), (dy, dx, 1)]
    value, gate, bc, step, cum, step_t, cum_t, decay, down, up = project(
        blocks,
        offsets,
        jnp.stack([2 * chip_at(dy, dx) + (core + o) % 2 for dy, dx, o in offsets]).astype(jnp.int32),
        complement,
        gate_proj,
        value_proj,
        state_proj,
        step_proj.T,
        step_bias.reshape(1, heads),
        decay_rate.reshape(1, heads),
    )
    comp_after, value = lax.optimization_barrier((complement, value))
    below = lax.ppermute(down, "seq", [(i, i + 1) for i in range(7)])
    above = lax.ppermute(up, "seq", [(i + 1, i) for i in range(7)])
    table = output_table(comp_after, core1, out_proj)
    below, above, *table = lax.optimization_barrier((below, above, *table))
    plain, plain_send, perm, perm_send = table
    tables = (plain, perm, to_sibling(plain_send), to_sibling(perm_send))
    pair_msg = jnp.where(half == 0, above[3:7, :128], below[3:7, :128])
    pair = jnp.stack([join(pair_msg[0], pair_msg[1]), join(pair_msg[2], pair_msg[3])])
    xs, end = conv_states(value, below, above, conv_kernel, bc, step, cum)

    d0 = jnp.where(half == 0, decay, pair)[:, :heads]
    d1 = jnp.where(half == 0, pair, decay)[:, :heads]

    def message(branch):
        parts = [*split(d0[branch]), *split(d1[branch])]
        rows4 = jnp.stack([jnp.pad(v, (0, 128 - heads)) for v in parts])
        rows4 = jnp.pad(rows4, ((0, 12), (0, 0)))
        return jnp.concatenate([end[branch].astype(BF).reshape(heads * 128, 128), rows4])

    msg_f, msg_b = message(0), message(1)
    got = []
    for k in range(1, 4):
        route = [(zz * 2 + hh, (zz + k) % 4 * 2 + hh) for zz in range(4) for hh in range(2)]
        got.append(lax.ppermute(jnp.where(z + k < 4, msg_f, msg_b), "seq", route))

    def opened(m):
        st = m[: heads * 128].astype(F32).reshape(heads, 128, 128)
        t = m[heads * 128 : heads * 128 + 4, :heads]
        return st, join(t[0], t[1]), join(t[2], t[3])

    opened_msgs = [opened(m) for m in got]
    wide = lambda v: v[:, None, None]

    def partial_sum(branch):
        total = jnp.zeros((heads, 128, 128), F32)
        passed = jnp.ones((heads,), F32)
        for j in range(1, 4):
            st, e0, e1 = opened_msgs[j - 1] if branch == 0 else opened_msgs[3 - j]
            valid = (z >= j) if branch == 0 else (z + j < 4)
            own_step = jnp.where(half == 0, e1, 1.0) if branch == 0 else jnp.where(half == 1, e0, 1.0)
            total = total + jnp.where(valid, wide(passed * own_step) * st, 0.0)
            passed = jnp.where(valid, passed * e0 * e1, passed)
        return total

    pf, pb = partial_sum(0), partial_sum(1)
    d0f, d1b = wide(d0[0]), wide(d1[1])
    send_f = jnp.where(half == 0, d0f * pf + end[0], pf)
    send_b = jnp.where(half == 1, d1b * pb + end[1], pb)
    recv = lax.ppermute(
        jnp.stack([send_f, send_b]).astype(BF), "seq", [(i, i ^ 1) for i in range(8)]
    ).astype(F32)
    in_f = jnp.where(half == 0, pf, d0f * pf) + recv[0]
    in_b = jnp.where(half == 1, pb, d1b * pb) + recv[1]
    incoming = jnp.stack([in_f, in_b]).astype(BF)

    local_y = within_shard(xs, bc, step_t, cum_t, cum, skip_gain.reshape(1, heads))
    normed = finish(local_y, incoming, bc, cum, gate, norm_gain.reshape(1, inner))
    others = to_sibling(normed)

    def shares(offsets, added=(), out_dtype=BF):
        order = jnp.stack([chip_at(dy, dx) for dy, dx in offsets]).astype(jnp.int32)
        return output_stage(order, normed, others, tables, added, out_dtype)

    r = to_chip(shares([(1, 2)])[0], 1, 0)
    s_a = to_chip(shares([(1, 1)])[0], 1, 0)
    s_b = to_chip(shares([(1, -1)])[0], 0, -1)
    s_c = to_chip(shares([(0, 2)], [(0, r)])[0], 0, 1)
    t_b = to_chip(shares([(0, -1)])[0], 0, -1)
    here = shares([(0, 0)], out_dtype=F32)[0]
    t_c = to_chip(shares([(1, 0)], [(0, s_b)])[0], 1, 0)
    t_a = to_chip(shares([(0, 1)], [(0, s_a), (0, s_c)])[0], 0, 1)
    summed = here + t_a.astype(F32) + t_b.astype(F32) + t_c.astype(F32)
    return (summed * keep_mask.astype(F32) * (1.0 / 0.9)).astype(BF)


def solution(mesh):
    return jax.shard_map(
        shards,
        mesh=mesh,
        in_specs=(
            P("seq", "chan"),
            P(None, "chan"),
            P(None, "chan"),
            P(),
            P(None, "chan"),
            P("chan"),
            P("chan"),
            P("chan"),
            P(None, "chan"),
            P("chan"),
            P("chan", None),
            P(),
            P("seq", "chan"),
        ),
        out_specs=P("seq", "chan"),
        check_vma=False,
    )
```

```python
import jax
import jax.numpy as jnp
from jax import lax
from jax.experimental import pallas as pl
from jax.experimental.pallas import tpu as pltpu
from jax.sharding import PartitionSpec as P

BF = jnp.bfloat16
F32 = jnp.float32
KW = 4


def chip_route(dy, dx):
    return [
        ((y * 4 + x) * 2 + c, ((y + dy) % 2 * 4 + (x + dx) % 4) * 2 + c)
        for y in range(2)
        for x in range(4)
        for c in range(2)
    ]


def to_chip(a, dy, dx):
    return lax.ppermute(a, "chan", chip_route(dy, dx))


def to_sibling(a):
    return lax.ppermute(a, "chan", [(i, i ^ 1) for i in range(16)])


def dot(a, b, dims=((1,), (0,)), precision=None):
    return lax.dot_general(
        a, b, (dims, ((), ())), preferred_element_type=F32, precision=precision
    )


def params(mib=24):
    return pltpu.CompilerParams(vmem_limit_bytes=mib * 2**20)


def cost(flops, nbytes):
    return pl.CostEstimate(flops=int(flops), bytes_accessed=int(nbytes), transcendentals=0)


def lanes(ref):
    row = ref[...]
    return jnp.concatenate([row, jnp.zeros((1, 128 - row.shape[1]), F32)], axis=1)


def project(blocks, offsets, place, comp, gate_proj, value_proj, state_proj, step_t, bias, rate):
    nb = len(blocks)
    rows, width = blocks[0].shape
    d = comp.shape[0]
    inner = gate_proj.shape[1]
    ns = state_proj.shape[1]
    heads = step_t.shape[0]
    tiles = rows // 128

    def kernel(place_ref, idx, *refs):
        chan = place_ref
        tok = refs[:nb]
        wg_hbm, wv_hbm, ws_hbm, st_ref, bias_ref, rate_ref = refs[nb : nb + 6]
        v_out, g_out, bc_out, step_o, cum_o, step_to, cum_to, decay_o, down_o, up_o = refs[nb + 6 : nb + 16]
        t, tp, by_row, picked, wg, wv, ws, sem, wsem = refs[nb + 16 :]

        def token_copy(j, at):
            return pltpu.make_async_copy(tok[j], t.at[:, pl.ds(at, width)], sem.at[j])

        weight_copies = [
            pltpu.make_async_copy(a, b, wsem.at[i])
            for i, (a, b) in enumerate([(ws_hbm, ws.at[:, :ns]), (wv_hbm, wv), (wg_hbm, wg)])
        ]
        for j in range(nb):
            token_copy(j, pl.multiple_of(chan[j] * width, width)).start()
        for c in weight_copies:
            c.start()
        st = st_ref[...].astype(F32)
        wst = jnp.concatenate([st, jnp.zeros((128 - heads, d), F32)], axis=0).T
        ws[:, ns:] = wst.astype(BF)

        for j in range(nb):
            at = pl.multiple_of(chan[j] * width, width)
            token_copy(j, at).wait()
            for k in range(tiles):
                part = t[128 * k : 128 * k + 128, pl.ds(at, width)].astype(F32).T
                by_row[pl.ds(at * tiles + k, width, tiles), :] = part

        def permute(weight, out, first):
            def body(i, _):
                cols = pl.ds(pl.multiple_of(i * 256, 256), 256)
                out[0, :, cols] = dot(t[...], weight[:, cols]).astype(BF)
                for c in range(4):
                    b0 = pl.multiple_of((first + i * 4 + c) * width, width)
                    base = c * width * tiles
                    for row in range(width):
                        src = pl.multiple_of(idx[b0 + row] * tiles, tiles)
                        picked[base + row * tiles : base + (row + 1) * tiles, :] = by_row[
                            pl.ds(src, tiles), :
                        ]
                    for k in range(tiles):
                        part = picked[pl.ds(base + k, width, tiles), :].T
                        tp[128 * k : 128 * k + 128, pl.ds(b0, width)] = part.astype(BF)
                return 0

            lax.fori_loop(0, 2, body, 0)

        weight_copies[1].wait()
        permute(wv, v_out, 0)
        weight_copies[2].wait()
        permute(wg, g_out, 8)
        weight_copies[0].wait()
        r = lax.broadcasted_iota(jnp.int32, (rows, rows), 0)
        q = lax.broadcasted_iota(jnp.int32, (rows, rows), 1)
        decays = []
        for b, u in enumerate((t, tp)):
            small = dot(u[...], ws[...])
            bc_out[b] = small[:, :ns].astype(BF)
            step = jax.nn.softplus(small[:, ns:] + lanes(bias_ref))
            tri = jnp.where((r >= q) if b == 0 else (r <= q), 1.0, 0.0).astype(BF)
            logdec = -step * lanes(rate_ref)
            high = logdec.astype(BF)
            rest = logdec - high.astype(F32)
            mid = rest.astype(BF)
            low = (rest - mid.astype(F32)).astype(BF)
            sums = dot(tri, jnp.concatenate([high, mid, low], axis=1))
            cum = sums[:, :128] + sums[:, 128:256] + sums[:, 256:]
            step_o[b] = step
            cum_o[b] = cum
            step_to[b] = step.T[:8]
            cum_to[b] = cum.T[:8]
            decay = jnp.exp(cum[rows - 1 : rows] if b == 0 else cum[0:1])
            decay_o[b : b + 1] = decay
            decays += [decay, decay - decay.astype(BF).astype(F32)]
        row8 = lax.broadcasted_iota(jnp.int32, (8, inner), 0)
        for b, u in enumerate((t, tp)):
            if b == 1:
                v_out[1] = dot(tp[...], wv[...]).astype(BF)
            edge = v_out[b, rows - 16 :] if b == 0 else v_out[b, :16]
            edge = edge.astype(F32)
            message = pltpu.roll(edge[8:], 3, 0) if b == 0 else edge[:8]
            for i, part in enumerate(decays):
                wide = jnp.concatenate([part, jnp.zeros((1, inner - 128), F32)], axis=1)
                message = jnp.where(row8 == 3 + i, wide, message)
            (down_o if b == 0 else up_o)[...] = message.astype(BF)
        g_out[1] = dot(tp[...], wg[...]).astype(BF)

    shapes = [
        jax.ShapeDtypeStruct((2, rows, inner), BF),
        jax.ShapeDtypeStruct((2, rows, inner), BF),
        jax.ShapeDtypeStruct((2, rows, ns), BF),
        jax.ShapeDtypeStruct((2, rows, 128), F32),
        jax.ShapeDtypeStruct((2, rows, 128), F32),
        jax.ShapeDtypeStruct((2, 8, rows), F32),
        jax.ShapeDtypeStruct((2, 8, rows), F32),
        jax.ShapeDtypeStruct((2, 128), F32),
        jax.ShapeDtypeStruct((8, inner), BF),
        jax.ShapeDtypeStruct((8, inner), BF),
    ]
    whole = lambda shape: pl.BlockSpec(shape, lambda n, s, i: (0,) * len(shape))
    any_spec = pl.BlockSpec(memory_space=pl.ANY)
    return pl.pallas_call(
        kernel,
        grid_spec=pltpu.PrefetchScalarGridSpec(
            num_scalar_prefetch=2,
            grid=(1,),
            in_specs=[any_spec] * (nb + 3) + [whole((heads, d)), whole((1, heads)), whole((1, heads))],
            out_specs=[whole(o.shape) for o in shapes],
            scratch_shapes=[
                pltpu.VMEM((rows, d), BF),
                pltpu.VMEM((rows, d), BF),
                pltpu.VMEM((d * tiles, 128), F32),
                pltpu.VMEM((4 * width * tiles, 128), F32),
                pltpu.VMEM((d, inner), BF),
                pltpu.VMEM((d, inner), BF),
                pltpu.VMEM((d, ns + 128), BF),
                pltpu.SemaphoreType.DMA((nb,)),
                pltpu.SemaphoreType.DMA((3,)),
            ],
        ),
        out_shape=shapes,
        compiler_params=params(60),
        cost_estimate=cost(4 * rows * d * (2 * inner + 512), 20 * 2**20),
        name="project",
    )(place, comp, *blocks, gate_proj, value_proj, state_proj, step_t, bias, rate)


def conv_states(value, below, above, taps, bc, step, cum):
    _, rows, inner = value.shape
    heads = inner // 128

    def kernel(v_ref, below_ref, above_ref, taps_ref, bc_ref, step_ref, cum_ref, xs_o, end_o):
        def branch(b):
            v = v_ref[0].astype(F32)
            if b == 0:
                padded = jnp.concatenate([pltpu.roll(below_ref[...].astype(F32), 5, 0), v], axis=0)
                shift = lambda k: padded[5 + k : 5 + k + rows]
            else:
                padded = jnp.concatenate([v, above_ref[...].astype(F32)], axis=0)
                shift = lambda k: padded[3 - k : 3 - k + rows]
            conv = taps_ref[0:1] * shift(0)
            for k in range(1, KW):
                conv = conv + taps_ref[k : k + 1] * shift(k)
            xs = (conv * jax.nn.sigmoid(conv)).astype(BF)
            xs_o[0] = xs
            cums = cum_ref[0]
            last = cums[rows - 1 : rows] if b == 0 else cums[0:1]
            towards = jnp.exp(last - cums) * step_ref[0]
            bm = bc_ref[0].astype(F32)
            for h in range(heads):
                weighted = (bm * towards[:, h : h + 1]).astype(BF)
                end_o[0, h] = dot(weighted, xs[:, h * 128 : h * 128 + 128], ((0,), (0,)))

        for b in range(2):
            pl.when(pl.program_id(0) == b)(lambda b=b: branch(b))

    by = lambda *shape: pl.BlockSpec((1, *shape), lambda b: (b,) + (0,) * len(shape))
    return pl.pallas_call(
        kernel,
        grid=(2,),
        in_specs=[
            by(rows, inner),
            pl.BlockSpec((8, inner), lambda b: (0, 0)),
            pl.BlockSpec((8, inner), lambda b: (0, 0)),
            pl.BlockSpec(taps.shape, lambda b: (0, 0)),
            by(rows, 128),
            by(rows, 128),
            by(rows, 128),
        ],
        out_specs=[by(rows, inner), by(heads, 128, 128)],
        out_shape=[
            jax.ShapeDtypeStruct((2, rows, inner), BF),
            jax.ShapeDtypeStruct((2, heads, 128, 128), F32),
        ],
        compiler_params=params(24),
        cost_estimate=cost(10**9, 3 * 2**20),
        name="conv_states",
    )(value, below, above, taps, bc, step, cum)


def within_shard(xs, bc, step_t, cum_t, cum, skip):
    _, rows, inner = xs.shape
    heads = inner // 128
    half = rows // 2

    def kernel(x_ref, bc_ref, st_ref, ct_ref, cum_ref, skip_ref, y_ref):
        h = pl.program_id(1)
        lane = lax.broadcasted_iota(jnp.int32, (1, 128), 1)
        pick = lane == h
        cum_col = jnp.sum(jnp.where(pick, cum_ref[0], 0.0), axis=1, keepdims=True)
        gain = jnp.sum(jnp.where(pick, lanes(skip_ref), 0.0), axis=1, keepdims=True)
        cum_row = ct_ref[0, pl.ds(h, 1), :]
        step_row = st_ref[0, pl.ds(h, 1), :]
        lower = lax.broadcasted_iota(jnp.int32, (half, half), 0) >= lax.broadcasted_iota(
            jnp.int32, (half, half), 1
        )
        upper = lax.broadcasted_iota(jnp.int32, (half, half), 0) <= lax.broadcasted_iota(
            jnp.int32, (half, half), 1
        )

        def part(t, s, mask):
            ts, ss = slice(t * half, t * half + half), slice(s * half, s * half + half)
            gap = jnp.minimum(cum_col[ts] - cum_row[:, ss], 0.0)
            w = jnp.exp(gap)
            if mask is not None:
                w = jnp.where(mask, w, 0.0)
            scores = dot(bc_ref[0, ts, 128:], bc_ref[0, ss, :128], ((1,), (1,)))
            mixing = (w * scores * step_row[:, ss]).astype(BF)
            return dot(mixing, x_ref[0, ss, :])

        def branch(b):
            early, late = (0, 1) if b == 0 else (1, 0)
            mask = lower if b == 0 else upper
            for t, y in (
                (early, part(early, early, mask)),
                (late, part(late, late, mask) + part(late, early, None)),
            ):
                ts = slice(t * half, t * half + half)
                y_ref[0, ts, :] = y + gain * x_ref[0, ts, :].astype(F32)

        for b in range(2):
            pl.when(pl.program_id(0) == b)(lambda b=b: branch(b))

    by = lambda *shape: pl.BlockSpec((1, *shape), lambda b, h: (b,) + (0,) * len(shape))
    head = pl.BlockSpec((1, rows, 128), lambda b, h: (b, 0, h))
    return pl.pallas_call(
        kernel,
        grid=(2, heads),
        in_specs=[
            head,
            by(rows, 256),
            by(8, rows),
            by(8, rows),
            by(rows, 128),
            pl.BlockSpec((1, heads), lambda b, h: (0, 0)),
        ],
        out_specs=head,
        out_shape=jax.ShapeDtypeStruct((2, rows, inner), F32),
        compiler_params=params(),
        cost_estimate=cost(4 * 10**9, 4 * 2**20),
        name="within_shard",
    )(xs, bc, step_t, cum_t, cum, skip)


def finish(local_y, incoming, bc, cum, gate, norm_gain):
    _, rows, inner = local_y.shape
    heads = inner // 128

    def kernel(y_ref, s_ref, bc_ref, cum_ref, g_ref, gain_ref, o_ref):
        h = pl.program_id(1)
        lane = lax.broadcasted_iota(jnp.int32, (1, 128), 1)
        cum_col = jnp.sum(jnp.where(lane == h, cum_ref[0], 0.0), axis=1, keepdims=True)
        entering = dot(bc_ref[0], s_ref[0, 0])
        y = y_ref[0] + jnp.exp(cum_col) * entering
        g = g_ref[0].astype(F32)
        gated = y * (g * jax.nn.sigmoid(g))
        scale = lax.rsqrt(jnp.mean(gated * gated, axis=-1, keepdims=True) + 1e-05)
        o_ref[...] = (gated * scale * gain_ref[...]).astype(BF)

    by = lambda *shape: pl.BlockSpec((1, *shape), lambda b, h: (b,) + (0,) * len(shape))
    head = pl.BlockSpec((1, rows, 128), lambda b, h: (b, 0, h))
    return pl.pallas_call(
        kernel,
        grid=(2, heads),
        in_specs=[
            head,
            pl.BlockSpec((1, 1, 128, 128), lambda b, h: (b, h, 0, 0)),
            pl.BlockSpec((1, rows, 128), lambda b, h: (b, 0, 1)),
            by(rows, 128),
            head,
            pl.BlockSpec((1, 128), lambda b, h: (0, h)),
        ],
        out_specs=pl.BlockSpec((rows, 128), lambda b, h: (0, b * heads + h)),
        out_shape=jax.ShapeDtypeStruct((rows, 2 * inner), BF),
        compiler_params=params(),
        cost_estimate=cost(10**9, 5 * 2**20),
        name="finish",
    )(local_y, incoming, bc, cum, gate, norm_gain)


def output_table(comp, core, out_proj):
    inner, d = out_proj.shape
    r = 512
    nb = d // r
    tiles = inner // 128
    half = r // 2

    def kernel(idx, core_ref, o_ref, plain_keep, plain_send, perm_keep, perm_send, rows_f32, picked):
        i = pl.program_id(0)
        even = core_ref[0] == 0

        def put(keep, send, j, t):
            keep[:, 128 * j : 128 * j + 128] = jnp.where(even, t[:half], t[half:]).astype(BF)
            send[:, 128 * j : 128 * j + 128] = jnp.where(even, t[half:], t[:half]).astype(BF)

        @pl.when(i < nb)
        def _():
            r0 = pl.multiple_of(i * r * tiles, r * tiles)
            for j in range(tiles):
                t = o_ref[128 * j : 128 * j + 128, :].astype(F32).T
                rows_f32[pl.ds(r0 + j, r, tiles), :] = t
                put(plain_keep, plain_send, j, t)

        @pl.when(i >= nb)
        def _():
            b0 = (i - nb) * r

            def body(n, _):
                for k in range(16):
                    row = n * 16 + k
                    src = pl.multiple_of(idx[b0 + row] * tiles, tiles)
                    dst = pl.multiple_of(row * tiles, tiles)
                    picked[pl.ds(dst, tiles), :] = rows_f32[pl.ds(src, tiles), :]
                return 0

            lax.fori_loop(0, r // 16, body, 0)
            for j in range(tiles):
                put(perm_keep, perm_send, j, picked[pl.ds(j, r, tiles), :])

    early = pl.BlockSpec((half, inner), lambda i, s, c: (jnp.minimum(i, nb - 1), 0))
    late = pl.BlockSpec((half, inner), lambda i, s, c: (jnp.maximum(i - nb, 0), 0))
    return pl.pallas_call(
        kernel,
        grid_spec=pltpu.PrefetchScalarGridSpec(
            num_scalar_prefetch=2,
            grid=(2 * nb,),
            in_specs=[pl.BlockSpec((inner, r), lambda i, s, c: (0, jnp.minimum(i, nb - 1)))],
            out_specs=[early, early, late, late],
            scratch_shapes=[
                pltpu.VMEM((d * tiles, 128), F32),
                pltpu.VMEM((r * tiles, 128), F32),
            ],
        ),
        out_shape=[jax.ShapeDtypeStruct((d // 2, inner), BF)] * 4,
        compiler_params=params(24),
        cost_estimate=cost(8 * 10**9, 12 * 2**20),
        name="output_table",
    )(comp, core, out_proj)


def output_stage(order, mine, others, tables, added, out_dtype):
    rows, twice = mine.shape
    inner = twice // 2
    n = order.shape[0]
    cols = 256
    na = len(added)

    def kernel(idx, a, b, p0, q0, p1, q1, *rest):
        o_ref = rest[na]
        nt = ((1,), (1,))
        left = jnp.concatenate([a[...], b[...]], axis=1)
        table = jnp.concatenate([p0[...], q0[...], p1[...], q1[...]], axis=1)
        total = dot(left, table, nt)
        for place in range(n):
            mask = pl.program_id(0) == place
            for (at, _), ref in zip(added, rest[:na]):
                if at == place and n == 1:
                    total = total + ref[...].astype(F32)
                elif at == place:
                    total = total + jnp.where(mask, ref[...].astype(F32), 0.0)
        o_ref[0] = total.astype(out_dtype)

    table = pl.BlockSpec((cols, inner), lambda i, s: (s[i], 0))
    whole = lambda c: pl.BlockSpec((rows, c), lambda i, s: (0, 0))
    return pl.pallas_call(
        kernel,
        grid_spec=pltpu.PrefetchScalarGridSpec(
            num_scalar_prefetch=1,
            grid=(n,),
            in_specs=[whole(twice), whole(twice)] + [table] * 4 + [whole(cols)] * na,
            out_specs=pl.BlockSpec((1, rows, cols), lambda i, s: (i, 0, 0)),
        ),
        out_shape=jax.ShapeDtypeStruct((n, rows, cols), out_dtype),
        compiler_params=params(24),
        cost_estimate=cost(n * 4 * rows * twice * cols, n * 3 * 2**20),
        name="output_stage",
    )(order, mine, others, *tables, *[v for _, v in added])


def split(a):
    high = a.astype(BF)
    return high, (a - high.astype(F32)).astype(BF)


def join(high, low):
    return high.astype(F32) + low.astype(F32)


def shards(
    tokens,
    gate_proj,
    value_proj,
    state_proj,
    step_proj,
    step_bias,
    decay_rate,
    skip_gain,
    conv_kernel,
    norm_gain,
    out_proj,
    complement,
    keep_mask,
):
    rows, width = tokens.shape
    inner = gate_proj.shape[1]
    heads = step_proj.shape[1]
    d = gate_proj.shape[0]
    place = lax.axis_index("chan")
    core, chip = place % 2, place // 2
    y, x = chip // 4, chip % 4
    seq = lax.axis_index("seq")
    z, half = seq // 2, seq % 2

    core1 = core.reshape(1).astype(jnp.int32)

    def chip_at(dy, dx):
        return (y + dy) % 2 * 4 + (x + dx) % 4

    own = tokens
    a = to_chip(own, 0, 1)
    b = to_chip(own, 0, -1)
    c = to_chip(own, 1, 0)
    own_s = to_sibling(own)
    a_s, b_s, c_s = to_sibling(a), to_sibling(b), to_sibling(c)
    dd = to_chip(a, 1, 0)
    e = to_chip(c, 0, -1)
    f = to_chip(a, 0, 1)
    g = to_chip(f, 1, 0)
    d_s, e_s, f_s = to_sibling(dd), to_sibling(e), to_sibling(f)
    g_s = to_sibling(g)
    parts = [
        (own, own_s, 0, 0),
        (a, a_s, 0, -1),
        (b, b_s, 0, 1),
        (c, c_s, 1, 0),
        (dd, d_s, 1, -1),
        (e, e_s, 1, 1),
        (f, f_s, 0, 2),
        (g, g_s, 1, 2),
    ]
    blocks, offsets = [], []
    for block, sib, dy, dx in parts:
        blocks += [block, sib]
        offsets += [(dy, dx, 0), (dy, dx, 1)]
    value, gate, bc, step, cum, step_t, cum_t, decay, down, up = project(
        blocks,
        offsets,
        jnp.stack([2 * chip_at(dy, dx) + (core + o) % 2 for dy, dx, o in offsets]).astype(jnp.int32),
        complement,
        gate_proj,
        value_proj,
        state_proj,
        step_proj.T,
        step_bias.reshape(1, heads),
        decay_rate.reshape(1, heads),
    )
    comp_after, value = lax.optimization_barrier((complement, value))
    below = lax.ppermute(down, "seq", [(i, i + 1) for i in range(7)])
    above = lax.ppermute(up, "seq", [(i + 1, i) for i in range(7)])
    table = output_table(comp_after, core1, out_proj)
    below, above, *table = lax.optimization_barrier((below, above, *table))
    plain, plain_send, perm, perm_send = table
    tables = (plain, perm, to_sibling(plain_send), to_sibling(perm_send))
    pair_msg = jnp.where(half == 0, above[3:7, :128], below[3:7, :128])
    pair = jnp.stack([join(pair_msg[0], pair_msg[1]), join(pair_msg[2], pair_msg[3])])
    xs, end = conv_states(value, below, above, conv_kernel, bc, step, cum)

    d0 = jnp.where(half == 0, decay, pair)[:, :heads]
    d1 = jnp.where(half == 0, pair, decay)[:, :heads]

    def message(branch):
        parts = [*split(d0[branch]), *split(d1[branch])]
        rows4 = jnp.stack([jnp.pad(v, (0, 128 - heads)) for v in parts])
        rows4 = jnp.pad(rows4, ((0, 12), (0, 0)))
        return jnp.concatenate([end[branch].astype(BF).reshape(heads * 128, 128), rows4])

    msg_f, msg_b = message(0), message(1)
    got = []
    for k in range(1, 4):
        route = [(zz * 2 + hh, (zz + k) % 4 * 2 + hh) for zz in range(4) for hh in range(2)]
        got.append(lax.ppermute(jnp.where(z + k < 4, msg_f, msg_b), "seq", route))

    def opened(m):
        st = m[: heads * 128].astype(F32).reshape(heads, 128, 128)
        t = m[heads * 128 : heads * 128 + 4, :heads]
        return st, join(t[0], t[1]), join(t[2], t[3])

    opened_msgs = [opened(m) for m in got]
    wide = lambda v: v[:, None, None]

    def partial_sum(branch):
        total = jnp.zeros((heads, 128, 128), F32)
        passed = jnp.ones((heads,), F32)
        for j in range(1, 4):
            st, e0, e1 = opened_msgs[j - 1] if branch == 0 else opened_msgs[3 - j]
            valid = (z >= j) if branch == 0 else (z + j < 4)
            own_step = jnp.where(half == 0, e1, 1.0) if branch == 0 else jnp.where(half == 1, e0, 1.0)
            total = total + jnp.where(valid, wide(passed * own_step) * st, 0.0)
            passed = jnp.where(valid, passed * e0 * e1, passed)
        return total

    pf, pb = partial_sum(0), partial_sum(1)
    d0f, d1b = wide(d0[0]), wide(d1[1])
    send_f = jnp.where(half == 0, d0f * pf + end[0], pf)
    send_b = jnp.where(half == 1, d1b * pb + end[1], pb)
    recv = lax.ppermute(
        jnp.stack([send_f, send_b]).astype(BF), "seq", [(i, i ^ 1) for i in range(8)]
    ).astype(F32)
    in_f = jnp.where(half == 0, pf, d0f * pf) + recv[0]
    in_b = jnp.where(half == 1, pb, d1b * pb) + recv[1]
    incoming = jnp.stack([in_f, in_b]).astype(BF)

    local_y = within_shard(xs, bc, step_t, cum_t, cum, skip_gain.reshape(1, heads))
    normed = finish(local_y, incoming, bc, cum, gate, norm_gain.reshape(1, inner))
    others = to_sibling(normed)

    def shares(offsets, added=(), out_dtype=BF):
        order = jnp.stack([chip_at(dy, dx) for dy, dx in offsets]).astype(jnp.int32)
        return output_stage(order, normed, others, tables, added, out_dtype)

    r = to_chip(shares([(1, 2)])[0], 1, 0)
    s_a = to_chip(shares([(1, 1)])[0], 1, 0)
    s_b = to_chip(shares([(1, -1)])[0], 0, -1)
    s_c = to_chip(shares([(0, 2)], [(0, r)])[0], 0, 1)
    t_b = to_chip(shares([(0, -1)])[0], 0, -1)
    here = shares([(0, 0)], out_dtype=F32)[0]
    t_c = to_chip(shares([(1, 0)], [(0, s_b)])[0], 1, 0)
    t_a = to_chip(shares([(0, 1)], [(0, s_a), (0, s_c)])[0], 0, 1)
    summed = here + t_a.astype(F32) + t_b.astype(F32) + t_c.astype(F32)
    return (summed * keep_mask.astype(F32) * (1.0 / 0.9)).astype(BF)


def solution(mesh):
    return jax.shard_map(
        shards,
        mesh=mesh,
        in_specs=(
            P("seq", "chan"),
            P(None, "chan"),
            P(None, "chan"),
            P(),
            P(None, "chan"),
            P("chan"),
            P("chan"),
            P("chan"),
            P(None, "chan"),
            P("chan"),
            P("chan", None),
            P(),
            P("seq", "chan"),
        ),
        out_specs=P("seq", "chan"),
        check_vma=False,
    )
```
